32 devices in a mesh: row: 8 (over y, x, core), vec: 4 (over z).
Axes of the slice: x: 2, y: 2, z: 4, core: 2. Of those that a mesh axis runs over, the one named last changes fastest.
Arguments:
- ham_tiles: bfloat16 [512, 4, 128, 128], P('row'), may hold values from -0.125 to 0.125
- tile_columns: int32 [512, 4], P('row'), may hold values from 0 to 511, as said below
- stack_lengths: int32 [8], P('row'), may hold values from 32 to 64, as said below
- start_vectors: bfloat16 [65536, 1024], P('row', 'vec'), may hold values from -6 to 6
- spectral_scale: float32 [1], replicated, may hold values from 4 to 16
Outputs:
- filtered_basis: bfloat16 [65536, 1024], P('row', 'vec')
The draws below stay inside these ranges and needn't reach their ends.
Inputs may be any that keep to these rules, and one draw needn't show every extreme that they name: `tile_columns`: row b lists 4 distinct block columns; the first is b itself, the others are (b + o) mod 512 with nonzero offsets o from -2 to 2. Some stack holds 64 occupied block rows and some other stack exactly half of 64; a stack's occupied rows are its first stack_lengths - 2 and its last 2 block rows.
All inputs are finite; a program needn't handle non-finite values.
Results may differ from the reference program's by a relative error of at most 0.006.
The reference program's roundings to bfloat16 on the way count: a program that leaves them out, or rounds other values in their place, can miss the bound.
Values may be sent and summed in bfloat16 or wider, within the bound.
A program may use at most 128 MiB of HBM per device.

```python
import math
import jax
import jax.numpy as jnp
from jax import lax

TILE = 128
NT = 4
REACH = 2
M = 1024
CHEB = 6
NS_ITERS = 2
BLK_DEV = 64
STACKS = 8
NB = 512
NR = 65536


def draw_tile_columns(key, part):
    block_ids = jnp.arange(NB, dtype=jnp.int32)
    offset_pool = jnp.array([-2, -1, 1, 2], dtype=jnp.int32)
    scores = jax.random.randint(key, (NB, 4), 0, 4096) * 4 + jnp.arange(4, dtype=jnp.int32)[None, :]
    ranking = jnp.argsort(scores, axis=1)
    chosen = offset_pool[ranking[:, :NT - 1]]
    offsets = jnp.concatenate([jnp.zeros((NB, 1), jnp.int32), chosen], axis=1)
    return ((block_ids[:, None] + offsets) % NB).astype(jnp.int32)


def draw_stack_lengths(key, part):
    key_full, key_uneven, key_first, key_second = jax.random.split(key, 4)
    full_flags = jax.random.randint(key_full, (STACKS,), 0, 2)
    uneven = jax.random.randint(key_uneven, (STACKS,), BLK_DEV // 2, BLK_DEV)
    counts = jnp.where(full_flags == 1, BLK_DEV, uneven)
    first_stack = jax.random.randint(key_first, (), 0, STACKS)
    second_stack = (first_stack + 1 + jax.random.randint(key_second, (), 0, STACKS - 1)) % STACKS
    counts = counts.at[first_stack].set(BLK_DEV).at[second_stack].set(BLK_DEV // 2)
    return counts.astype(jnp.int32)


def draw_start_vectors(key, part):
    key_entries = jax.random.fold_in(key, 71)
    values = jnp.clip(jax.random.normal(key_entries, (NR, M), jnp.float32), -6.0, 6.0)
    return values.astype(jnp.bfloat16)


def level_of(key, dims, cuts, least, top_value):
    def one(dim, parts):
        steps = jax.random.uniform(jax.random.fold_in(jax.random.fold_in(key, 6), dim), (parts,), jnp.float32, least / len(cuts), top_value / len(cuts))
        return jnp.repeat(jnp.exp(steps), dims[dim] // parts).reshape((-1,) + (1,) * (len(dims) - dim - 1))

    loudness = one(*cuts[0])
    for cut in cuts[1:]:
        loudness = loudness * one(*cut)
    return loudness


def gaussian(key, dims, spread, most, pieces=(), kind=jnp.bfloat16):
    values = spread * jax.random.normal(key, dims, jnp.float32)
    if pieces:
        values = values * level_of(key, dims, pieces, -0.22, 0.18)
    return jnp.clip(values, -most, most).astype(kind)


def setup_inputs(seed: int = 0) -> dict:
    keys = jax.random.split(jax.random.key(seed), 6)
    return {
        "ham_tiles": gaussian(keys[0], (NB, NT, TILE, TILE), (4 * NT * TILE) ** -0.5, 0.125, ((0, 8),)),
        "tile_columns": draw_tile_columns(jax.random.fold_in(keys[5], 71), 0),
        "stack_lengths": draw_stack_lengths(jax.random.fold_in(keys[5], 71), 0),
        "start_vectors": draw_start_vectors(jax.random.fold_in(keys[5], 71), 0),
        "spectral_scale": jnp.clip(jnp.exp(jax.random.uniform(keys[4], (1,), jnp.float32, math.log(4.0), math.log(16.0))), 4.0, 16.0),
    }


def apply_hamiltonian(ham_tiles, tile_columns, stack_lengths, current):
    blocked = current.reshape(NB, TILE, M)

    def group_product(group):
        start = (group * BLK_DEV).astype(jnp.int32)
        tile_group = lax.dynamic_slice_in_dim(ham_tiles, start, BLK_DEV, 0).astype(jnp.float32)
        column_group = lax.dynamic_slice_in_dim(tile_columns, start, BLK_DEV, 0)
        picked = blocked[column_group].astype(jnp.float32)
        product = jnp.einsum('btij,btjc->bic', tile_group, picked)
        local_rows = jnp.arange(BLK_DEV, dtype=jnp.int32)
        live = (local_rows < stack_lengths[group] - REACH) | (local_rows >= BLK_DEV - REACH)
        live_rows = live.astype(jnp.float32)
        return product * live_rows[:, None, None]
    stacked = lax.map(group_product, jnp.arange(STACKS, dtype=jnp.int32))
    return stacked.reshape(NR, M)

def reference(ham_tiles, tile_columns, stack_lengths, start_vectors, spectral_scale):
    earlier = start_vectors
    current = apply_hamiltonian(ham_tiles, tile_columns, stack_lengths, start_vectors).astype(jnp.bfloat16)
    for repeat in range(CHEB - 1):
        image = apply_hamiltonian(ham_tiles, tile_columns, stack_lengths, current)
        following = (2.0 * image - earlier.astype(jnp.float32)).astype(jnp.bfloat16)
        earlier, current = (current, following)
    filtered = current.astype(jnp.float32)
    gram = lax.dot_general(filtered, filtered, (((0,), (0,)), ((), ())), precision=lax.Precision.HIGHEST) / NR
    scale = spectral_scale[0] * jnp.trace(gram) / M
    system = gram / scale
    root = jnp.eye(M, dtype=jnp.float32)
    for repeat in range(NS_ITERS):
        product_w = jnp.dot(system, root, precision=lax.Precision.HIGHEST)
        product_p = jnp.dot(product_w, root, precision=lax.Precision.HIGHEST)
        root = 1.5 * root - 0.5 * jnp.dot(product_p, root, precision=lax.Precision.HIGHEST)
    weights = (root / jnp.sqrt(scale)).astype(jnp.bfloat16)
    basis = jnp.dot(filtered, weights.astype(jnp.float32), precision=lax.Precision.HIGHEST)
    return basis.astype(jnp.bfloat16)
```

```python
import functools

import jax
import jax.numpy as jnp
from jax import lax
from jax.experimental import pallas as pl
from jax.experimental.pallas import tpu as pltpu
from jax.sharding import PartitionSpec as P

REACH = 2
CHEB = 6
MESH = pl.DeviceIdType.MESH


def packed_rows(panels, width, count):
    unit = 16 * count * panels
    return -(-(panels * (panels + 1) // 2 * width) // unit) * unit


def mirrored_groups(groups):
    return groups * 3 // 8


def step_kernel(
    total_blocks,
    total_rows,
    columns_ref,
    lengths_ref,
    spectral_ref,
    tiles_hbm,
    start_hbm,
    out_ref,
    start,
    even,
    odd,
    final,
    halo,
    prim,
    sec,
    acc,
    arrived,
    outgoing,
    total,
    near,
    thin,
    far,
    summed,
    load_sem,
    halo_send,
    halo_recv,
    prim_send,
    prim_recv,
    prim_keep,
    sec_send,
    sec_recv,
    sec_keep,
    gram_send,
    gram_recv,
    back_send,
    back_recv,
    mate_send,
    mate_recv,
):
    block_count, tile_count, tile, _ = tiles_hbm.shape
    groups, panels, pair, width = prim.shape
    mirrored = sec.shape[0]
    pairs = groups * panels
    half = panels // 2
    full = panels * width
    count = lax.axis_size("row")
    me, vec = lax.axis_index("row"), lax.axis_index("vec")
    left, right = lax.rem(me + count - 1, count), lax.rem(me + 1, count)
    vec_at = [lax.rem(vec + d, panels) for d in range(panels)]
    upper, low = vec // half, lax.rem(vec, half)
    mates = [upper * half + lax.rem(low + e, half) for e in range(half)]
    across = [(1 - upper) * half + lax.rem(low + e, half) for e in range(half)]
    c = pairs // 2
    waves = c - CHEB - 1

    def rows_of(p):
        return pl.ds(pl.multiple_of(p * pair, pair), pair)

    def remote(source, target, send, recv, device):
        return pltpu.make_async_remote_copy(
            src_ref=source,
            dst_ref=target,
            send_sem=send,
            recv_sem=recv,
            device_id=device,
            device_id_type=MESH,
        )

    barrier = pltpu.get_barrier_semaphore()
    greeted = [{"row": lax.rem(me + d, count)} for d in range(1, count)]
    greeted += [{"vec": place} for place in vec_at[1:]]
    for device in greeted:
        pl.semaphore_signal(barrier, inc=1, device_id=device, device_id_type=MESH)

    def halo_copies(source, step):
        return (
            remote(
                source.at[pl.ds(0, pair)],
                halo.at[step, 1],
                halo_send.at[step, 1],
                halo_recv.at[step, 1],
                {"row": left},
            ),
            remote(
                source.at[pl.ds((pairs - 1) * pair, pair)],
                halo.at[step, 0],
                halo_send.at[step, 0],
                halo_recv.at[step, 0],
                {"row": right},
            ),
        )

    def prim_copy(g, d):
        return remote(
            final.at[rows_of(g * panels + vec_at[d])],
            prim.at[g, vec],
            prim_send.at[g, d - 1],
            prim_recv.at[g, d - 1],
            {"vec": vec_at[d]},
        )

    def prim_local(g):
        return pltpu.make_async_copy(
            final.at[rows_of(g * panels + vec)], prim.at[g, vec], prim_keep.at[g]
        )

    def send_chunk(p):
        g, owner = p // panels, lax.rem(p, panels)
        d = lax.rem(owner - vec + panels, panels)

        @pl.when(d != 0)
        def _():
            remote(
                final.at[rows_of(p)],
                prim.at[g, vec],
                prim_send.at[g, d - 1],
                prim_recv.at[g, d - 1],
                {"vec": owner},
            ).start()

        @pl.when(d == 0)
        def _():
            prim_local(g).start()

    def sec_copy(g, d):
        return remote(
            final.at[rows_of(g * panels + panels - 1 - vec_at[d])],
            sec.at[g, vec],
            sec_send.at[g, d - 1],
            sec_recv.at[g, d - 1],
            {"vec": vec_at[d]},
        )

    def sec_local(g):
        return pltpu.make_async_copy(
            final.at[rows_of(g * panels + panels - 1 - vec)], sec.at[g, vec], sec_keep.at[g]
        )

    def mirror(g):
        for d in range(1, panels):
            sec_copy(g, d).start()
        sec_local(g).start()

    def filter_scope(tiles, band):
        def tile_load(n, lo, hi):
            piece = pl.ds(lo * REACH, (hi - lo) * REACH)
            return pltpu.make_async_copy(tiles_hbm.at[piece], tiles.at[piece], load_sem.at[n])

        def start_load(n, lo, hi):
            piece = pl.ds(lo * pair, (hi - lo) * pair)
            return pltpu.make_async_copy(start_hbm.at[piece], start.at[piece], load_sem.at[n])

        first = [tile_load(0, c - CHEB, c + CHEB), start_load(1, c - CHEB - 1, c + CHEB + 1)]
        rest = [
            start_load(2, 0, c - CHEB - 1),
            start_load(3, c + CHEB + 1, pairs),
            tile_load(4, 0, c - CHEB),
            tile_load(5, c + CHEB, pairs),
        ]
        for load in first + rest:
            load.start()

        def build(p):
            for i in range(REACH):
                b = p * REACH + i
                live = (b < lengths_ref[0] - REACH) | (b >= block_count - REACH)
                places = []
                for t in range(1, tile_count):
                    shift = lax.rem(
                        columns_ref[b, t] - (me * block_count + b) + REACH + total_blocks,
                        total_blocks,
                    )
                    places.append(jnp.where(live, shift, -1))

                def masked(t, hit):
                    mask = jnp.where(hit, 1.0, 0.0).astype(jnp.float32)
                    mask = jnp.full((tile, tile), mask, jnp.float32).astype(jnp.bfloat16)
                    return tiles[b, t] * mask

                for k in range(3 * REACH):
                    if k - i == REACH:
                        value = masked(0, live)
                    elif 0 <= k - i <= 2 * REACH:
                        value = masked(1, places[0] == k - i)
                        for t in range(2, tile_count):
                            value = value + masked(t, places[t - 1] == k - i)
                    else:
                        value = jnp.zeros((tile, tile), jnp.bfloat16)
                    band[p, i * tile : (i + 1) * tile, k * tile : (k + 1) * tile] = value

        held = [start] + [(odd, even)[step % 2] for step in range(CHEB - 1)] + [final]

        def finish(step, product, rows):
            if step:
                product = 2.0 * product - held[step - 1][rows, :].astype(jnp.float32)
            held[step + 1][rows, :] = product.astype(jnp.bfloat16)

        def interior(step, p):
            before = pl.multiple_of((p - 1) * pair, pair)
            finish(
                step,
                jnp.dot(
                    band[p],
                    held[step][pl.ds(before, 3 * pair), :],
                    preferred_element_type=jnp.float32,
                ),
                rows_of(p),
            )

        for load in first:
            load.wait()

        def base(n, carry):
            for p in (c - 1 - n, c + n):
                build(p)
                interior(0, p)
            return carry

        lax.fori_loop(0, CHEB, base, 0)
        for step in range(1, CHEB):

            def layer(n, carry, step=step):
                interior(step, c - 1 - n)
                interior(step, c + n)
                return carry

            lax.fori_loop(0, CHEB - step, layer, 0)

        pl.semaphore_wait(barrier, len(greeted))
        send_chunk(c)
        send_chunk(c - 1)
        for load in rest:
            load.wait()
        copies = halo_copies(start, 0)
        for copy in copies:
            copy.start()

        def wave(i, carry):
            build(c + CHEB - 1 + i)
            build(c - CHEB - i)
            for step in range(CHEB):
                interior(step, c + CHEB - 1 - step + i)
                interior(step, c - CHEB + step - i)
            send_chunk(c + i)
            send_chunk(c - 1 - i)
            return carry

        lax.fori_loop(1, waves + 1, wave, 0)
        build(0)
        build(pairs - 1)

        last = (pairs - 1) * pair
        for step in range(CHEB):
            current = held[step]
            for copy in copies:
                copy.wait()
            finish(
                step,
                jnp.dot(band[0, :, :pair], halo[step, 0], preferred_element_type=jnp.float32)
                + jnp.dot(
                    band[0, :, pair:], current[0 : 2 * pair, :], preferred_element_type=jnp.float32
                ),
                pl.ds(0, pair),
            )
            finish(
                step,
                jnp.dot(
                    band[pairs - 1, :, 2 * pair :],
                    halo[step, 1],
                    preferred_element_type=jnp.float32,
                )
                + jnp.dot(
                    band[pairs - 1, :, : 2 * pair],
                    current[last - pair : last + pair, :],
                    preferred_element_type=jnp.float32,
                ),
                pl.ds(last, pair),
            )
            if step < CHEB - 1:
                copies = halo_copies(held[step + 1], step + 1)
                for copy in copies:
                    copy.start()
            else:
                send_chunk(pairs - 1)
                send_chunk(0)

            def sides(p, carry, step=step):
                interior(step, p)
                interior(step, pairs - 1 - p)
                if step == CHEB - 1:
                    send_chunk(p)
                    send_chunk(pairs - 1 - p)
                return carry

            lax.fori_loop(1, 1 + step, sides, 0)

    pl.run_scoped(
        filter_scope,
        pltpu.VMEM((block_count, tile_count, tile, tile), jnp.bfloat16),
        pltpu.VMEM((pairs, pair, 3 * pair), jnp.bfloat16),
    )

    acc[...] = jnp.zeros_like(acc)

    def accumulate(g):
        for d in range(1, panels):
            prim_copy(g, d).wait_recv()
        prim_local(g).wait()
        n = 0
        for i in range(panels):
            for j in range(i + 1):
                acc[n * width : (n + 1) * width, :] += lax.dot_general(
                    prim[g, j],
                    prim[g, i],
                    (((0,), (0,)), ((), ())),
                    preferred_element_type=jnp.float32,
                )
                n += 1

    def both(n, carry):
        accumulate(groups // 2 + n)
        accumulate(groups // 2 - 1 - n)
        return carry

    lax.fori_loop(0, groups // 2 - 1, both, 0)
    accumulate(groups - 1)
    early = min(1, mirrored)
    for g in range(early):
        mirror(g)
    accumulate(0)

    side, quad, quads = lax.rem(me, 2), me // 2, count // 2
    other = 1 - side
    packed = acc.shape[0]
    part = packed // 2
    slab = part // quads
    height = slab // panels
    quad_at = [lax.rem(quad + d, quads) for d in range(quads)]
    slots = iter(range(2 + 2 * (quads - 1) + 2 * (panels - 1)))

    def span(at, size):
        return pl.ds(pl.multiple_of(at, 16), size)

    def gram_copy(source, target, device):
        slot = next(slots)
        copy = remote(source, target, gram_send.at[slot], gram_recv.at[slot], device)
        copy.start()
        return copy

    gram_copy(acc.at[span(other * part, part)], arrived, {"row": quad * 2 + other}).wait()
    for d in range(1, quads):
        at = quad_at[d] * slab
        outgoing[d - 1] = (
            (acc[span(side * part + at, slab), :] + arrived[span(at, slab), :])
            * (1.0 / total_rows)
        ).astype(jnp.bfloat16)
    copies = [
        gram_copy(outgoing.at[d - 1], near.at[d - 1], {"row": quad_at[d] * 2 + side})
        for d in range(1, quads)
    ]
    at = quad * slab
    total[...] = (acc[span(side * part + at, slab), :] + arrived[span(at, slab), :]) * (
        1.0 / total_rows
    )
    for d in range(1, quads):
        copies[d - 1].wait()
        total[...] += near[d - 1].astype(jnp.float32)

    thin[...] = total[...].astype(jnp.bfloat16)
    copies = [
        gram_copy(thin.at[span(vec_at[d] * height, height)], far.at[d - 1], {"vec": vec_at[d]})
        for d in range(1, panels)
    ]
    reduced = total[span(vec * height, height), :]
    for d in range(1, panels):
        copies[d - 1].wait()
        reduced += far[d - 1].astype(jnp.float32)
    at = side * part + quad * slab
    mine = span(at + vec * height, height)
    summed[mine, :] = reduced.astype(jnp.bfloat16)
    mine = summed.at[mine]
    copies = [gram_copy(mine, mine, {"vec": place}) for place in vec_at[1:]]
    for copy in copies:
        copy.wait()
    for g in range(early, mirrored):
        mirror(g)
    mine = summed.at[span(at, slab)]
    copies = [gram_copy(mine, mine, {"row": place * 2 + side}) for place in quad_at[1:]]
    for copy in copies:
        copy.wait()
    mine = summed.at[span(side * part, part)]
    gram_copy(mine, mine, {"row": quad * 2 + other}).wait()

    def basis_scope(gram, high, low_side, base, weights):
        diagonal = lax.broadcasted_iota(jnp.int32, (width, width), 0) == lax.broadcasted_iota(
            jnp.int32, (width, width), 1
        )
        trace = jnp.zeros((1, 1), jnp.float32)
        for i in range(panels):
            n = i * (i + 1) // 2 + i
            block = summed[n * width : (n + 1) * width, :].astype(jnp.float32)
            trace += jnp.sum(jnp.where(diagonal, block, 0.0), axis=(0, 1), keepdims=True)
        scale = spectral_ref[0] * trace / float(full)
        rest, factor = scale, jnp.ones((1, 1), jnp.float32)
        for k in (64, 32, 16, 8, 4, 2, 1):
            up, down = 2.0**k, 2.0**-k
            big = rest >= up
            rest, factor = jnp.where(big, rest * down, rest), jnp.where(big, factor * down, factor)
            small = rest < down
            rest, factor = jnp.where(small, rest * up, rest), jnp.where(small, factor * up, factor)
        inverse = 1.0 / rest
        shrink = 1.0 / jnp.sqrt(scale)
        n = 0
        for i in range(panels):
            for j in range(i + 1):
                wide = summed[n * width : (n + 1) * width, :].astype(jnp.float32) * factor
                n += 1
                gram[j * width : (j + 1) * width, i * width : (i + 1) * width] = wide.astype(
                    jnp.bfloat16
                )
                if i != j:
                    gram[i * width : (i + 1) * width, j * width : (j + 1) * width] = (
                        wide.T.astype(jnp.bfloat16)
                    )

        def squares(r, carry):
            rows = pl.ds(pl.multiple_of(r * width, width), width)
            square = jnp.dot(gram[rows, :], gram[...], preferred_element_type=jnp.float32)
            square = square * inverse * inverse
            system = gram[rows, :].astype(jnp.float32) * inverse
            high[rows, :] = square.astype(jnp.bfloat16)
            low_side[rows, :] = (0.0625 * square - 0.5625 * system).astype(jnp.bfloat16)
            ones = lax.broadcasted_iota(jnp.int32, (width, full), 0) + r * width
            ones = ones == lax.broadcasted_iota(jnp.int32, (width, full), 1)
            base[rows, :] = jnp.where(ones, 2.25, 0.0) - 2.4375 * system + 1.6875 * square
            return carry

        lax.fori_loop(0, panels, squares, 0)

        def products(r, carry):
            rows = pl.ds(pl.multiple_of(r * width, width), width)
            product = jnp.dot(high[rows, :], low_side[...], preferred_element_type=jnp.float32)
            root = (base[rows, :] + product) * shrink
            for v in range(panels):
                weights[v, rows, :] = root[:, v * width : (v + 1) * width].astype(jnp.bfloat16)
            return carry

        lax.fori_loop(0, panels, products, 0)

        def product(chunk, place):
            value = None
            for u in range(panels):
                term = jnp.dot(
                    chunk[u],
                    weights[place, u * width : (u + 1) * width, :],
                    preferred_element_type=jnp.float32,
                )
                value = term if value is None else value + term
            return value.astype(jnp.bfloat16)

        hops = across + mates[1:]

        def back_copy(g, k):
            slot = (g - mirrored) * (panels - 1) + k
            return remote(
                even.at[rows_of(slot)],
                out_ref.at[rows_of(g * panels + vec)],
                back_send.at[slot],
                back_recv.at[slot],
                {"vec": hops[k]},
            )

        def plain_task(g):
            chunk = prim.at[g]
            for k in range(panels - 1):
                slot = (g - mirrored) * (panels - 1) + k
                even[rows_of(slot), :] = product(chunk, hops[k])
                back_copy(g, k).start()
            out_ref[rows_of(g * panels + vec), :] = product(chunk, vec)

        held_slots = (groups - mirrored) * (panels - 1)

        def mate_copy(g, role, e):
            place = g * panels + (panels - 1 - vec if role else vec)
            slot = (role * mirrored + g) * (half - 1) + e - 1
            return remote(
                even.at[rows_of(held_slots + slot)],
                out_ref.at[rows_of(place)],
                mate_send.at[slot],
                mate_recv.at[slot],
                {"vec": mates[e]},
            )

        def mirror_task(g, role):
            chunk = sec.at[g] if role else prim.at[g]
            if role:
                for d in range(1, panels):
                    sec_copy(g, d).wait_recv()
                sec_local(g).wait()
            place = g * panels + (panels - 1 - vec if role else vec)
            for e in range(1, half):
                slot = (role * mirrored + g) * (half - 1) + e - 1
                even[rows_of(held_slots + slot), :] = product(chunk, mates[e])
                mate_copy(g, role, e).start()
            out_ref[rows_of(place), :] = product(chunk, vec)

        plain = groups - mirrored
        shared = min(plain, mirrored)

        def first_round(n, carry):
            plain_task(mirrored + n)
            mirror_task(n, 0)
            return carry

        lax.fori_loop(0, shared, first_round, 0)

        def second_round(n, carry):
            plain_task(mirrored + shared + n)
            mirror_task(n, 1)
            return carry

        again = min(plain - shared, mirrored)
        lax.fori_loop(0, again, second_round, 0)

        def only_plain(n, carry):
            plain_task(n)
            return carry

        lax.fori_loop(mirrored + shared + again, groups, only_plain, 0)

        def only_mirror(n, carry):
            mirror_task(n, 1)
            return carry

        lax.fori_loop(again, mirrored, only_mirror, 0)

        def close_prim(g, carry):
            for d in range(1, panels):
                prim_copy(g, d).wait_send()
            return carry

        lax.fori_loop(0, groups, close_prim, 0)

        def close_mirror(g, carry):
            for d in range(1, panels):
                sec_copy(g, d).wait_send()
            for role in range(2):
                for e in range(1, half):
                    mate_copy(g, role, e).wait()
            return carry

        lax.fori_loop(0, mirrored, close_mirror, 0)

        def close_back(g, carry):
            for k in range(panels - 1):
                back_copy(g, k).wait()
            return carry

        lax.fori_loop(mirrored, groups, close_back, 0)

    square = (full, full)
    pl.run_scoped(
        basis_scope,
        pltpu.VMEM(square, jnp.bfloat16),
        pltpu.VMEM(square, jnp.bfloat16),
        pltpu.VMEM(square, jnp.bfloat16),
        pltpu.VMEM(square, jnp.float32),
        pltpu.VMEM((panels, full, width), jnp.bfloat16),
    )


def local(ham_tiles, tile_columns, stack_lengths, start_vectors, spectral_scale):
    block_count, _, tile, _ = ham_tiles.shape
    rows, width = start_vectors.shape
    count, panels = lax.axis_size("row"), lax.axis_size("vec")
    pair = REACH * tile
    pairs = block_count // REACH
    groups = pairs // panels
    mirrored = mirrored_groups(groups)
    quads, half = count // 2, panels // 2
    packed = packed_rows(panels, width, count)
    part = packed // 2
    slab = part // quads
    height = slab // panels
    vmem = pl.BlockSpec(memory_space=pltpu.VMEM)
    smem = pl.BlockSpec(memory_space=pltpu.SMEM)
    hbm = pl.BlockSpec(memory_space=pl.ANY)
    gram_copies = 2 + 2 * (quads - 1) + 2 * (panels - 1)
    back = (groups - mirrored) * (panels - 1)
    mate = 2 * mirrored * (half - 1)
    dma = pltpu.SemaphoreType.DMA
    return pl.pallas_call(
        functools.partial(step_kernel, block_count * count, rows * count),
        out_shape=jax.ShapeDtypeStruct((rows, width), jnp.bfloat16),
        in_specs=[smem, smem, smem, hbm, hbm],
        out_specs=vmem,
        scratch_shapes=[
            pltpu.VMEM((rows, width), jnp.bfloat16),
            pltpu.VMEM((rows, width), jnp.bfloat16),
            pltpu.VMEM((rows, width), jnp.bfloat16),
            pltpu.VMEM((rows, width), jnp.bfloat16),
            pltpu.VMEM((CHEB, 2, pair, width), jnp.bfloat16),
            pltpu.VMEM((groups, panels, pair, width), jnp.bfloat16),
            pltpu.VMEM((mirrored, panels, pair, width), jnp.bfloat16),
            pltpu.VMEM((packed, width), jnp.float32),
            pltpu.VMEM((part, width), jnp.float32),
            pltpu.VMEM((quads - 1, slab, width), jnp.bfloat16),
            pltpu.VMEM((slab, width), jnp.float32),
            pltpu.VMEM((quads - 1, slab, width), jnp.bfloat16),
            pltpu.VMEM((slab, width), jnp.bfloat16),
            pltpu.VMEM((panels - 1, height, width), jnp.bfloat16),
            pltpu.VMEM((packed, width), jnp.bfloat16),
            dma((6,)),
            dma((CHEB, 2)),
            dma((CHEB, 2)),
            dma((groups, panels - 1)),
            dma((groups, panels - 1)),
            dma((groups,)),
            dma((mirrored, panels - 1)),
            dma((mirrored, panels - 1)),
            dma((mirrored,)),
            dma((gram_copies,)),
            dma((gram_copies,)),
            dma((back,)),
            dma((back,)),
            dma((mate,)),
            dma((mate,)),
        ],
        compiler_params=pltpu.CompilerParams(
            collective_id=0, has_side_effects=True, vmem_limit_bytes=56 * 1024 * 1024
        ),
    )(tile_columns, stack_lengths, spectral_scale, ham_tiles, start_vectors)


def solution(mesh):
    placed = (P("row", None, None, None), P("row", None), P("row"), P("row", "vec"), P())
    return jax.shard_map(
        local, mesh=mesh, in_specs=placed, out_specs=P("row", "vec"), check_vma=False
    )
```

```python
import functools

import jax
import jax.numpy as jnp
from jax import lax
from jax.experimental import pallas as pl
from jax.experimental.pallas import tpu as pltpu
from jax.sharding import PartitionSpec as P

REACH = 2
CHEB = 6
MESH = pl.DeviceIdType.MESH


def packed_rows(panels, width, count):
    unit = 16 * count * panels
    return -(-(panels * (panels + 1) // 2 * width) // unit) * unit


def mirrored_groups(groups):
    return groups * 3 // 8


def step_kernel(
    total_blocks,
    total_rows,
    columns_ref,
    lengths_ref,
    spectral_ref,
    tiles_hbm,
    start_hbm,
    out_ref,
    start,
    even,
    odd,
    final,
    halo,
    prim,
    sec,
    arrived,
    near,
    far,
    summed,
    load_sem,
    halo_send,
    halo_recv,
    prim_send,
    prim_recv,
    prim_keep,
    sec_send,
    sec_recv,
    sec_keep,
    gram_send,
    gram_recv,
    back_send,
    back_recv,
    plain_keep,
    mate_send,
    mate_recv,
    mate_keep,
):
    block_count, tile_count, tile, _ = tiles_hbm.shape
    groups, panels, pair, width = prim.shape
    mirrored = sec.shape[0]
    pairs = groups * panels
    half = panels // 2
    full = panels * width
    count = lax.axis_size("row")
    me, vec = lax.axis_index("row"), lax.axis_index("vec")
    left, right = lax.rem(me + count - 1, count), lax.rem(me + 1, count)
    vec_at = [lax.rem(vec + d, panels) for d in range(panels)]
    upper, low = vec // half, lax.rem(vec, half)
    mates = [upper * half + lax.rem(low + e, half) for e in range(half)]
    across = [(1 - upper) * half + lax.rem(low + e, half) for e in range(half)]
    c = pairs // 2
    spare = c - 2 * CHEB
    part, quads = arrived.shape[0], count // 2
    packed, slab = 2 * part, part // quads
    height = slab // panels

    def rows_of(p):
        return pl.ds(pl.multiple_of(p * pair, pair), pair)

    def remote(source, target, send, recv, device):
        return pltpu.make_async_remote_copy(
            src_ref=source,
            dst_ref=target,
            send_sem=send,
            recv_sem=recv,
            device_id=device,
            device_id_type=MESH,
        )

    barrier = pltpu.get_barrier_semaphore()
    greeted = [{"row": lax.rem(me + d, count)} for d in range(1, count)]
    greeted += [{"vec": place} for place in vec_at[1:]]
    for device in greeted:
        pl.semaphore_signal(barrier, inc=1, device_id=device, device_id_type=MESH)

    def halo_copies(source, step):
        return (
            remote(
                source.at[pl.ds(0, pair)],
                halo.at[step, 1],
                halo_send.at[step, 1],
                halo_recv.at[step, 1],
                {"row": left},
            ),
            remote(
                source.at[pl.ds((pairs - 1) * pair, pair)],
                halo.at[step, 0],
                halo_send.at[step, 0],
                halo_recv.at[step, 0],
                {"row": right},
            ),
        )

    def prim_copy(g, d):
        return remote(
            final.at[rows_of(g * panels + vec_at[d])],
            prim.at[g, vec],
            prim_send.at[g, d - 1],
            prim_recv.at[g, d - 1],
            {"vec": vec_at[d]},
        )

    def prim_local(g):
        return pltpu.make_async_copy(
            final.at[rows_of(g * panels + vec)], prim.at[g, vec], prim_keep.at[g]
        )

    def send_chunk(p):
        g, owner = p // panels, lax.rem(p, panels)
        d = lax.rem(owner - vec + panels, panels)

        @pl.when(d != 0)
        def _():
            remote(
                final.at[rows_of(p)],
                prim.at[g, vec],
                prim_send.at[g, d - 1],
                prim_recv.at[g, d - 1],
                {"vec": owner},
            ).start()

        @pl.when(d == 0)
        def _():
            prim_local(g).start()

    mirror_order = [(g, d) for g in range(mirrored) for d in range(1, panels)]
    first_part = panels - 1

    def sec_copy(g, d):
        return remote(
            final.at[rows_of(g * panels + panels - 1 - vec_at[d])],
            sec.at[g, vec],
            sec_send.at[g, d - 1],
            sec_recv.at[g, d - 1],
            {"vec": vec_at[d]},
        )

    def sec_local(g):
        return pltpu.make_async_copy(
            final.at[rows_of(g * panels + panels - 1 - vec)], sec.at[g, vec], sec_keep.at[g]
        )

    def mirror(lo, hi):
        for g, d in mirror_order[lo:hi]:
            sec_copy(g, d).start()

    def filter_scope(tiles, band):
        def tile_load(n, lo, hi, slot):
            return pltpu.make_async_copy(
                tiles_hbm.at[pl.ds(lo * REACH, (hi - lo) * REACH)],
                tiles.at[pl.ds(slot * REACH, (hi - lo) * REACH)],
                load_sem.at[n],
            )

        def start_load(n, lo, hi):
            piece = pl.ds(lo * pair, (hi - lo) * pair)
            return pltpu.make_async_copy(start_hbm.at[piece], start.at[piece], load_sem.at[n])

        first = [
            tile_load(0, c - CHEB, c + CHEB, 0),
            start_load(1, c - CHEB - 1, c + CHEB + 1),
        ]
        rest = [
            start_load(2, 0, c - CHEB - 1),
            start_load(3, c + CHEB + 1, pairs),
            tile_load(4, CHEB, c - CHEB, 2 * CHEB),
            tile_load(5, c + CHEB, pairs - CHEB, 2 * CHEB + spare),
        ]
        ends = [tile_load(6, 0, CHEB, 0), tile_load(7, pairs - CHEB, pairs, CHEB)]
        for load in first + rest:
            load.start()

        def build(p, slot):
            for i in range(REACH):
                b = p * REACH + i
                at = slot * REACH + i
                live = (b < lengths_ref[0] - REACH) | (b >= block_count - REACH)
                places = []
                for t in range(1, tile_count):
                    shift = lax.rem(
                        columns_ref[t, b] - (me * block_count + b) + REACH + total_blocks,
                        total_blocks,
                    )
                    places.append(jnp.where(live, shift, -1))

                def masked(t, hit):
                    mask = jnp.where(hit, 1.0, 0.0).astype(jnp.float32)
                    mask = jnp.full((tile, tile), mask, jnp.float32).astype(jnp.bfloat16)
                    return tiles[at, t] * mask

                for k in range(3 * REACH):
                    if k - i == REACH:
                        value = masked(0, live)
                    elif 0 <= k - i <= 2 * REACH:
                        value = masked(1, places[0] == k - i)
                        for t in range(2, tile_count):
                            value = value + masked(t, places[t - 1] == k - i)
                    else:
                        value = jnp.zeros((tile, tile), jnp.bfloat16)
                    band[p, i * tile : (i + 1) * tile, k * tile : (k + 1) * tile] = value

        held = [start] + [(odd, even)[step % 2] for step in range(CHEB - 1)] + [final]

        def finish(step, product, rows):
            if step:
                product = 2.0 * product - held[step - 1][rows, :].astype(jnp.float32)
            held[step + 1][rows, :] = product.astype(jnp.bfloat16)

        def interior(step, p):
            before = pl.multiple_of((p - 1) * pair, pair)
            finish(
                step,
                jnp.dot(
                    band[p],
                    held[step][pl.ds(before, 3 * pair), :],
                    preferred_element_type=jnp.float32,
                ),
                rows_of(p),
            )

        for load in first:
            load.wait()

        def base(n, carry):
            for p in (c - 1 - n, c + n):
                build(p, p - (c - CHEB))
                interior(0, p)
            return carry

        lax.fori_loop(0, CHEB, base, 0)
        for load in ends:
            load.start()
        for step in range(1, CHEB):

            def layer(n, carry, step=step):
                interior(step, c - 1 - n)
                interior(step, c + n)
                return carry

            lax.fori_loop(0, CHEB - step, layer, 0)

        pl.semaphore_wait(barrier, len(greeted))
        send_chunk(c)
        send_chunk(c - 1)
        for load in rest + ends:
            load.wait()
        copies = halo_copies(start, 0)
        for copy in copies:
            copy.start()

        last = (pairs - 1) * pair

        def waves(lo, hi):
            first_step = max(0, -(-(lo - spare) // 2))

            def wave(i, carry):
                if first_step == 0:
                    build(c + CHEB - 1 + i, 2 * CHEB + spare - 1 + i)
                    build(c - CHEB - i, 2 * CHEB + spare - i)
                for step in range(first_step, CHEB):
                    interior(step, c + CHEB - 1 - step + i)
                    interior(step, c - CHEB + step - i)
                send_chunk(c + i)
                send_chunk(c - 1 - i)
                return carry

            lax.fori_loop(lo, hi, wave, 0)

        def edges(step, copies):
            current = held[step]
            if step == 0:

                def outer(p, carry):
                    build(p, p)
                    build(pairs - 1 - p, 2 * CHEB - 1 - p)
                    return carry

                lax.fori_loop(0, CHEB, outer, 0)
            for copy in copies:
                copy.wait()
            finish(
                step,
                jnp.dot(band[0, :, :pair], halo[step, 0], preferred_element_type=jnp.float32)
                + jnp.dot(
                    band[0, :, pair:], current[0 : 2 * pair, :], preferred_element_type=jnp.float32
                ),
                pl.ds(0, pair),
            )
            finish(
                step,
                jnp.dot(
                    band[pairs - 1, :, 2 * pair :],
                    halo[step, 1],
                    preferred_element_type=jnp.float32,
                )
                + jnp.dot(
                    band[pairs - 1, :, : 2 * pair],
                    current[last - pair : last + pair, :],
                    preferred_element_type=jnp.float32,
                ),
                pl.ds(last, pair),
            )
            if step == CHEB - 1:
                send_chunk(pairs - 1)
                send_chunk(0)
                return []
            copies = halo_copies(held[step + 1], step + 1)
            for copy in copies:
                copy.start()

            def sides(p, carry, step=step):
                interior(step, p)
                interior(step, pairs - 1 - p)
                return carry

            lax.fori_loop(1, CHEB - step, sides, 0)
            return copies

        waves(1, 2)
        copies = edges(0, copies)
        waves(2, spare)
        copies = edges(1, copies)
        waves(spare, spare + 1)
        for step in range(CHEB - 1):
            waves(spare + 1 + 2 * step, spare + 3 + 2 * step)
            if step + 2 < CHEB:
                copies = edges(step + 2, copies)

    pl.run_scoped(
        filter_scope,
        pltpu.VMEM((2 * (CHEB + spare) * REACH, tile_count, tile, tile), jnp.bfloat16),
        pltpu.VMEM((pairs, pair, 3 * pair), jnp.bfloat16),
    )

    def basis_scope(acc, outgoing, total, thin, gram, high, low_side, base, weights):
        acc[...] = jnp.zeros_like(acc)

        def accumulate(g):
            for d in range(1, panels):
                prim_copy(g, d).wait_recv()
            prim_local(g).wait()
            n = 0
            for i in range(panels):
                for j in range(i + 1):
                    acc[n * width : (n + 1) * width, :] += lax.dot_general(
                        prim[g, j],
                        prim[g, i],
                        (((0,), (0,)), ((), ())),
                        preferred_element_type=jnp.float32,
                    )
                    n += 1

        def both(n, carry):
            accumulate(groups // 2 + n)
            accumulate(groups // 2 - 1 - n)
            return carry

        lax.fori_loop(0, groups // 2 - 1, both, 0)
        accumulate(groups - 1)
        mirror(0, first_part)
        for g in range(mirrored):
            sec_local(g).start()
        accumulate(0)

        side, quad = lax.rem(me, 2), me // 2
        other = 1 - side
        quad_at = [lax.rem(quad + d, quads) for d in range(quads)]
        slots = iter(range(2 + 2 * (quads - 1) + 2 * (panels - 1)))

        def span(at, size):
            return pl.ds(pl.multiple_of(at, 16), size)

        def gram_copy(source, target, device):
            slot = next(slots)
            copy = remote(source, target, gram_send.at[slot], gram_recv.at[slot], device)
            copy.start()
            return copy

        gram_copy(acc.at[span(other * part, part)], arrived, {"row": quad * 2 + other}).wait()
        for d in range(1, quads):
            at = quad_at[d] * slab
            outgoing[d - 1] = (
                (acc[span(side * part + at, slab), :] + arrived[span(at, slab), :])
                * (1.0 / total_rows)
            ).astype(jnp.bfloat16)
        copies = [
            gram_copy(outgoing.at[d - 1], near.at[d - 1], {"row": quad_at[d] * 2 + side})
            for d in range(1, quads)
        ]
        at = quad * slab
        total[...] = (acc[span(side * part + at, slab), :] + arrived[span(at, slab), :]) * (
            1.0 / total_rows
        )
        for d in range(1, quads):
            copies[d - 1].wait()
            total[...] += near[d - 1].astype(jnp.float32)

        thin[...] = total[...].astype(jnp.bfloat16)
        copies = [
            gram_copy(thin.at[span(vec_at[d] * height, height)], far.at[d - 1], {"vec": vec_at[d]})
            for d in range(1, panels)
        ]
        reduced = total[span(vec * height, height), :]
        for d in range(1, panels):
            copies[d - 1].wait()
            reduced += far[d - 1].astype(jnp.float32)
        at = side * part + quad * slab
        mine = span(at + vec * height, height)
        summed[mine, :] = reduced.astype(jnp.bfloat16)
        mine = summed.at[mine]
        copies = [gram_copy(mine, mine, {"vec": place}) for place in vec_at[1:]]
        for copy in copies:
            copy.wait()
        mirror(first_part, len(mirror_order))
        mine = summed.at[span(at, slab)]
        copies = [gram_copy(mine, mine, {"row": place * 2 + side}) for place in quad_at[1:]]
        for copy in copies:
            copy.wait()
        mine = summed.at[span(side * part, part)]
        gram_copy(mine, mine, {"row": quad * 2 + other}).wait()

        diagonal = lax.broadcasted_iota(jnp.int32, (width, width), 0) == lax.broadcasted_iota(
            jnp.int32, (width, width), 1
        )
        trace = jnp.zeros((1, 1), jnp.float32)
        for i in range(panels):
            n = i * (i + 1) // 2 + i
            block = summed[n * width : (n + 1) * width, :].astype(jnp.float32)
            trace += jnp.sum(jnp.where(diagonal, block, 0.0), axis=(0, 1), keepdims=True)
        scale = spectral_ref[0] * trace / float(full)
        rest, factor = scale, jnp.ones((1, 1), jnp.float32)
        for k in (64, 32, 16, 8, 4, 2, 1):
            up, down = 2.0**k, 2.0**-k
            big = rest >= up
            rest, factor = jnp.where(big, rest * down, rest), jnp.where(big, factor * down, factor)
            small = rest < down
            rest, factor = jnp.where(small, rest * up, rest), jnp.where(small, factor * up, factor)
        inverse = 1.0 / rest
        shrink = 1.0 / jnp.sqrt(scale)
        n = 0
        for i in range(panels):
            for j in range(i + 1):
                wide = summed[n * width : (n + 1) * width, :].astype(jnp.float32) * factor
                n += 1
                gram[j * width : (j + 1) * width, i * width : (i + 1) * width] = wide.astype(
                    jnp.bfloat16
                )
                if i != j:
                    gram[i * width : (i + 1) * width, j * width : (j + 1) * width] = (
                        wide.T.astype(jnp.bfloat16)
                    )

        def squares(r, carry):
            rows = pl.ds(pl.multiple_of(r * width, width), width)
            square = jnp.dot(gram[rows, :], gram[...], preferred_element_type=jnp.float32)
            square = square * inverse * inverse
            system = gram[rows, :].astype(jnp.float32) * inverse
            high[rows, :] = square.astype(jnp.bfloat16)
            low_side[rows, :] = (0.0625 * square - 0.5625 * system).astype(jnp.bfloat16)
            ones = lax.broadcasted_iota(jnp.int32, (width, full), 0) + r * width
            ones = ones == lax.broadcasted_iota(jnp.int32, (width, full), 1)
            base[rows, :] = jnp.where(ones, 2.25, 0.0) - 2.4375 * system + 1.6875 * square
            return carry

        lax.fori_loop(0, panels, squares, 0)

        def products(r, carry):
            rows = pl.ds(pl.multiple_of(r * width, width), width)
            product = jnp.dot(high[rows, :], low_side[...], preferred_element_type=jnp.float32)
            root = (base[rows, :] + product) * shrink
            for v in range(panels):
                weights[v, rows, :] = root[:, v * width : (v + 1) * width].astype(jnp.bfloat16)
            return carry

        lax.fori_loop(0, panels, products, 0)

        def product(chunk, place):
            value = None
            for u in range(panels):
                term = jnp.dot(
                    chunk[u],
                    weights[place, u * width : (u + 1) * width, :],
                    preferred_element_type=jnp.float32,
                )
                value = term if value is None else value + term
            return value.astype(jnp.bfloat16)

        hops = across + mates[1:]

        def back_copy(g, k):
            slot = (g - mirrored) * (panels - 1) + k
            return remote(
                even.at[rows_of(slot)],
                out_ref.at[rows_of(g * panels + vec)],
                back_send.at[slot],
                back_recv.at[slot],
                {"vec": hops[k]},
            )

        plain_slots = (groups - mirrored) * (panels - 1)

        def plain_local(g):
            return pltpu.make_async_copy(
                even.at[rows_of(plain_slots + g - mirrored)],
                out_ref.at[rows_of(g * panels + vec)],
                plain_keep.at[g - mirrored],
            )

        def plain_task(g):
            chunk = prim.at[g]
            for k in range(panels - 1):
                slot = (g - mirrored) * (panels - 1) + k
                even[rows_of(slot), :] = product(chunk, hops[k])
                back_copy(g, k).start()
            even[rows_of(plain_slots + g - mirrored), :] = product(chunk, vec)
            plain_local(g).start()

        held_slots = (groups - mirrored) * panels
        mate_slots = held_slots + 2 * mirrored * (half - 1)

        def mate_copy(g, role, e):
            place = g * panels + (panels - 1 - vec if role else vec)
            slot = (role * mirrored + g) * (half - 1) + e - 1
            return remote(
                even.at[rows_of(held_slots + slot)],
                out_ref.at[rows_of(place)],
                mate_send.at[slot],
                mate_recv.at[slot],
                {"vec": mates[e]},
            )

        def mate_local(g, role):
            place = g * panels + (panels - 1 - vec if role else vec)
            return pltpu.make_async_copy(
                even.at[rows_of(mate_slots + role * mirrored + g)],
                out_ref.at[rows_of(place)],
                mate_keep.at[role * mirrored + g],
            )

        def mirror_task(g, role):
            chunk = sec.at[g] if role else prim.at[g]
            if role:
                for d in range(1, panels):
                    sec_copy(g, d).wait_recv()
                sec_local(g).wait()
            for e in range(1, half):
                slot = (role * mirrored + g) * (half - 1) + e - 1
                even[rows_of(held_slots + slot), :] = product(chunk, mates[e])
                mate_copy(g, role, e).start()
            even[rows_of(mate_slots + role * mirrored + g), :] = product(chunk, vec)
            mate_local(g, role).start()

        plain = groups - mirrored
        shared = min(plain, mirrored)

        def first_round(n, carry):
            plain_task(mirrored + n)
            mirror_task(n, 0)
            return carry

        lax.fori_loop(0, shared, first_round, 0)

        def second_round(n, carry):
            plain_task(mirrored + shared + n)
            mirror_task(n, 1)
            return carry

        again = min(plain - shared, mirrored)
        lax.fori_loop(0, again, second_round, 0)

        def only_plain(n, carry):
            plain_task(n)
            return carry

        lax.fori_loop(mirrored + shared + again, groups, only_plain, 0)

        def only_mirror(n, carry):
            mirror_task(n, 1)
            return carry

        lax.fori_loop(again, mirrored, only_mirror, 0)

        def close_prim(g, carry):
            for d in range(1, panels):
                prim_copy(g, d).wait_send()
            return carry

        lax.fori_loop(0, groups, close_prim, 0)

        def close_mirror(g, carry):
            for d in range(1, panels):
                sec_copy(g, d).wait_send()
            for role in range(2):
                for e in range(1, half):
                    mate_copy(g, role, e).wait()
                mate_local(g, role).wait()
            return carry

        lax.fori_loop(0, mirrored, close_mirror, 0)

        def close_back(g, carry):
            for k in range(panels - 1):
                back_copy(g, k).wait()
            plain_local(g).wait()
            return carry

        lax.fori_loop(mirrored, groups, close_back, 0)

    square = (full, full)
    pl.run_scoped(
        basis_scope,
        pltpu.VMEM((packed, width), jnp.float32),
        pltpu.VMEM((quads - 1, slab, width), jnp.bfloat16),
        pltpu.VMEM((slab, width), jnp.float32),
        pltpu.VMEM((slab, width), jnp.bfloat16),
        pltpu.VMEM(square, jnp.bfloat16),
        pltpu.VMEM(square, jnp.bfloat16),
        pltpu.VMEM(square, jnp.bfloat16),
        pltpu.VMEM(square, jnp.float32),
        pltpu.VMEM((panels, full, width), jnp.bfloat16),
    )


def local(ham_tiles, tile_columns, stack_lengths, start_vectors, spectral_scale):
    block_count, _, tile, _ = ham_tiles.shape
    rows, width = start_vectors.shape
    count, panels = lax.axis_size("row"), lax.axis_size("vec")
    pair = REACH * tile
    pairs = block_count // REACH
    groups = pairs // panels
    mirrored = mirrored_groups(groups)
    quads, half = count // 2, panels // 2
    packed = packed_rows(panels, width, count)
    part = packed // 2
    slab = part // quads
    height = slab // panels
    smem = pl.BlockSpec(memory_space=pltpu.SMEM)
    hbm = pl.BlockSpec(memory_space=pl.ANY)
    gram_copies = 2 + 2 * (quads - 1) + 2 * (panels - 1)
    back = (groups - mirrored) * (panels - 1)
    mate = 2 * mirrored * (half - 1)
    dma = pltpu.SemaphoreType.DMA
    return pl.pallas_call(
        functools.partial(step_kernel, block_count * count, rows * count),
        out_shape=jax.ShapeDtypeStruct((rows, width), jnp.bfloat16),
        in_specs=[smem, smem, smem, hbm, hbm],
        out_specs=pl.BlockSpec(memory_space=pltpu.HBM),
        scratch_shapes=[
            pltpu.VMEM((rows, width), jnp.bfloat16),
            pltpu.VMEM((rows, width), jnp.bfloat16),
            pltpu.VMEM((rows, width), jnp.bfloat16),
            pltpu.VMEM((rows, width), jnp.bfloat16),
            pltpu.VMEM((CHEB, 2, pair, width), jnp.bfloat16),
            pltpu.VMEM((groups, panels, pair, width), jnp.bfloat16),
            pltpu.VMEM((mirrored, panels, pair, width), jnp.bfloat16),
            pltpu.VMEM((part, width), jnp.float32),
            pltpu.VMEM((quads - 1, slab, width), jnp.bfloat16),
            pltpu.VMEM((panels - 1, height, width), jnp.bfloat16),
            pltpu.VMEM((packed, width), jnp.bfloat16),
            dma((8,)),
            dma((CHEB, 2)),
            dma((CHEB, 2)),
            dma((groups, panels - 1)),
            dma((groups, panels - 1)),
            dma((groups,)),
            dma((mirrored, panels - 1)),
            dma((mirrored, panels - 1)),
            dma((mirrored,)),
            dma((gram_copies,)),
            dma((gram_copies,)),
            dma((back,)),
            dma((back,)),
            dma((groups - mirrored,)),
            dma((mate,)),
            dma((mate,)),
            dma((2 * mirrored,)),
        ],
        compiler_params=pltpu.CompilerParams(
            collective_id=0, has_side_effects=True, vmem_limit_bytes=47 * 1024 * 1024
        ),
    )(tile_columns.T, stack_lengths, spectral_scale, ham_tiles, start_vectors)


def solution(mesh):
    placed = (P("row", None, None, None), P("row", None), P("row"), P("row", "vec"), P())
    return jax.shard_map(
        local, mesh=mesh, in_specs=placed, out_specs=P("row", "vec"), check_vma=False
    )
```

```python
import functools

import jax
import jax.numpy as jnp
from jax import lax
from jax.experimental import pallas as pl
from jax.experimental.pallas import tpu as pltpu
from jax.sharding import PartitionSpec as P

REACH = 2
CHEB = 6
MESH = pl.DeviceIdType.MESH


def packed_rows(panels, width, count):
    unit = 16 * count * panels
    return -(-(panels * (panels + 1) // 2 * width) // unit) * unit


def mirrored_groups(groups):
    return groups * 3 // 8


def step_kernel(
    total_blocks,
    total_rows,
    columns_ref,
    lengths_ref,
    spectral_ref,
    tiles_hbm,
    start_hbm,
    out_ref,
    start,
    even,
    odd,
    final,
    halo,
    prim,
    sec,
    arrived,
    near,
    far,
    summed,
    load_sem,
    halo_send,
    halo_recv,
    prim_send,
    prim_recv,
    prim_keep,
    sec_send,
    sec_recv,
    sec_keep,
    gram_send,
    gram_recv,
    back_send,
    back_recv,
    plain_keep,
    mate_send,
    mate_recv,
    mate_keep,
):
    block_count, tile_count, tile, _ = tiles_hbm.shape
    groups, panels, pair, width = prim.shape
    mirrored = sec.shape[0]
    pairs = groups * panels
    half = panels // 2
    full = panels * width
    count = lax.axis_size("row")
    me, vec = lax.axis_index("row"), lax.axis_index("vec")
    left, right = lax.rem(me + count - 1, count), lax.rem(me + 1, count)
    vec_at = [lax.rem(vec + d, panels) for d in range(panels)]
    upper, low = vec // half, lax.rem(vec, half)
    mates = [upper * half + lax.rem(low + e, half) for e in range(half)]
    across = [(1 - upper) * half + lax.rem(low + e, half) for e in range(half)]
    c = pairs // 2
    spare = c - 2 * CHEB
    part, quads = arrived.shape[0], count // 2
    packed, slab = 2 * part, part // quads
    height = slab // panels

    def rows_of(p):
        return pl.ds(pl.multiple_of(p * pair, pair), pair)

    def remote(source, target, send, recv, device):
        return pltpu.make_async_remote_copy(
            src_ref=source,
            dst_ref=target,
            send_sem=send,
            recv_sem=recv,
            device_id=device,
            device_id_type=MESH,
        )

    barrier = pltpu.get_barrier_semaphore()
    greeted = [{"row": lax.rem(me + d, count)} for d in range(1, count)]
    greeted += [{"vec": place} for place in vec_at[1:]]
    for device in greeted:
        pl.semaphore_signal(barrier, inc=1, device_id=device, device_id_type=MESH)

    def halo_copies(source, step):
        return (
            remote(
                source.at[pl.ds(0, pair)],
                halo.at[step, 1],
                halo_send.at[step, 1],
                halo_recv.at[step, 1],
                {"row": left},
            ),
            remote(
                source.at[pl.ds((pairs - 1) * pair, pair)],
                halo.at[step, 0],
                halo_send.at[step, 0],
                halo_recv.at[step, 0],
                {"row": right},
            ),
        )

    def prim_copy(g, d):
        return remote(
            final.at[rows_of(g * panels + vec_at[d])],
            prim.at[g, vec],
            prim_send.at[g, d - 1],
            prim_recv.at[g, d - 1],
            {"vec": vec_at[d]},
        )

    def prim_local(g):
        return pltpu.make_async_copy(
            final.at[rows_of(g * panels + vec)], prim.at[g, vec], prim_keep.at[g]
        )

    def send_chunk(p):
        g, owner = p // panels, lax.rem(p, panels)
        d = lax.rem(owner - vec + panels, panels)

        @pl.when(d != 0)
        def _():
            remote(
                final.at[rows_of(p)],
                prim.at[g, vec],
                prim_send.at[g, d - 1],
                prim_recv.at[g, d - 1],
                {"vec": owner},
            ).start()

        @pl.when(d == 0)
        def _():
            prim_local(g).start()

    mirror_order = [(g, d) for g in range(mirrored) for d in range(1, panels)]
    first_part = panels - 1

    def sec_copy(g, d):
        return remote(
            final.at[rows_of(g * panels + panels - 1 - vec_at[d])],
            sec.at[g, vec],
            sec_send.at[g, d - 1],
            sec_recv.at[g, d - 1],
            {"vec": vec_at[d]},
        )

    def sec_local(g):
        return pltpu.make_async_copy(
            final.at[rows_of(g * panels + panels - 1 - vec)], sec.at[g, vec], sec_keep.at[g]
        )

    def mirror(lo, hi):
        for g, d in mirror_order[lo:hi]:
            sec_copy(g, d).start()

    def filter_scope(tiles, band):
        def tile_load(n, lo, hi, slot):
            return pltpu.make_async_copy(
                tiles_hbm.at[pl.ds(lo * REACH, (hi - lo) * REACH)],
                tiles.at[pl.ds(slot * REACH, (hi - lo) * REACH)],
                load_sem.at[n],
            )

        def start_load(n, lo, hi):
            piece = pl.ds(lo * pair, (hi - lo) * pair)
            return pltpu.make_async_copy(start_hbm.at[piece], start.at[piece], load_sem.at[n])

        first = [
            tile_load(0, c - CHEB, c + CHEB, 0),
            start_load(1, c - CHEB - 1, c + CHEB + 1),
        ]
        rest = [
            start_load(2, 0, c - CHEB - 1),
            start_load(3, c + CHEB + 1, pairs),
            tile_load(4, CHEB, c - CHEB, 2 * CHEB),
            tile_load(5, c + CHEB, pairs - CHEB, 2 * CHEB + spare),
        ]
        ends = [tile_load(6, 0, CHEB, 0), tile_load(7, pairs - CHEB, pairs, CHEB)]
        for load in first + rest:
            load.start()

        def build(p, slot):
            for i in range(REACH):
                b = p * REACH + i
                at = slot * REACH + i
                live = (b < lengths_ref[0] - REACH) | (b >= block_count - REACH)
                places = []
                for t in range(1, tile_count):
                    shift = lax.rem(
                        columns_ref[t, b] - (me * block_count + b) + REACH + total_blocks,
                        total_blocks,
                    )
                    places.append(jnp.where(live, shift, -1))

                def masked(t, hit):
                    mask = jnp.where(hit, 1.0, 0.0).astype(jnp.float32)
                    mask = jnp.full((tile, tile), mask, jnp.float32).astype(jnp.bfloat16)
                    return tiles[at, t] * mask

                for k in range(3 * REACH):
                    if k - i == REACH:
                        value = masked(0, live)
                    elif 0 <= k - i <= 2 * REACH:
                        value = masked(1, places[0] == k - i)
                        for t in range(2, tile_count):
                            value = value + masked(t, places[t - 1] == k - i)
                    else:
                        value = jnp.zeros((tile, tile), jnp.bfloat16)
                    band[p, i * tile : (i + 1) * tile, k * tile : (k + 1) * tile] = value

        held = [start] + [(odd, even)[step % 2] for step in range(CHEB - 1)] + [final]

        def finish(step, product, rows):
            if step:
                product = 2.0 * product - held[step - 1][rows, :].astype(jnp.float32)
            held[step + 1][rows, :] = product.astype(jnp.bfloat16)

        def interior(step, p):
            before = pl.multiple_of((p - 1) * pair, pair)
            finish(
                step,
                jnp.dot(
                    band[p],
                    held[step][pl.ds(before, 3 * pair), :],
                    preferred_element_type=jnp.float32,
                ),
                rows_of(p),
            )

        for load in first:
            load.wait()

        def base(n, carry):
            for p in (c - 1 - n, c + n):
                build(p, p - (c - CHEB))
                interior(0, p)
            return carry

        lax.fori_loop(0, CHEB, base, 0)
        for load in ends:
            load.start()
        for step in range(1, CHEB):

            def layer(n, carry, step=step):
                interior(step, c - 1 - n)
                interior(step, c + n)
                return carry

            lax.fori_loop(0, CHEB - step, layer, 0)

        pl.semaphore_wait(barrier, len(greeted))
        send_chunk(c)
        send_chunk(c - 1)
        for load in rest + ends:
            load.wait()
        copies = halo_copies(start, 0)
        for copy in copies:
            copy.start()

        last = (pairs - 1) * pair

        def waves(lo, hi):
            first_step = max(0, -(-(lo - spare) // 2))

            def wave(i, carry):
                if first_step == 0:
                    build(c + CHEB - 1 + i, 2 * CHEB + spare - 1 + i)
                    build(c - CHEB - i, 2 * CHEB + spare - i)
                for step in range(first_step, CHEB):
                    interior(step, c + CHEB - 1 - step + i)
                    interior(step, c - CHEB + step - i)
                send_chunk(c + i)
                send_chunk(c - 1 - i)
                return carry

            lax.fori_loop(lo, hi, wave, 0)

        def edges(step, copies):
            current = held[step]
            if step == 0:

                def outer(p, carry):
                    build(p, p)
                    build(pairs - 1 - p, 2 * CHEB - 1 - p)
                    return carry

                lax.fori_loop(0, CHEB, outer, 0)
            for copy in copies:
                copy.wait()
            finish(
                step,
                jnp.dot(band[0, :, :pair], halo[step, 0], preferred_element_type=jnp.float32)
                + jnp.dot(
                    band[0, :, pair:], current[0 : 2 * pair, :], preferred_element_type=jnp.float32
                ),
                pl.ds(0, pair),
            )
            finish(
                step,
                jnp.dot(
                    band[pairs - 1, :, 2 * pair :],
                    halo[step, 1],
                    preferred_element_type=jnp.float32,
                )
                + jnp.dot(
                    band[pairs - 1, :, : 2 * pair],
                    current[last - pair : last + pair, :],
                    preferred_element_type=jnp.float32,
                ),
                pl.ds(last, pair),
            )
            if step == CHEB - 1:
                send_chunk(pairs - 1)
                send_chunk(0)
                return []
            copies = halo_copies(held[step + 1], step + 1)
            for copy in copies:
                copy.start()

            def sides(p, carry, step=step):
                interior(step, p)
                interior(step, pairs - 1 - p)
                return carry

            lax.fori_loop(1, CHEB - step, sides, 0)
            return copies

        waves(1, 2)
        copies = edges(0, copies)
        waves(2, spare)
        copies = edges(1, copies)
        waves(spare, spare + 1)
        for step in range(CHEB - 1):
            waves(spare + 1 + 2 * step, spare + 3 + 2 * step)
            if step + 2 < CHEB:
                copies = edges(step + 2, copies)

    pl.run_scoped(
        filter_scope,
        pltpu.VMEM((2 * (CHEB + spare) * REACH, tile_count, tile, tile), jnp.bfloat16),
        pltpu.VMEM((pairs, pair, 3 * pair), jnp.bfloat16),
    )

    def basis_scope(acc, outgoing, total, thin, gram, high, low_side, base, weights):
        acc[...] = jnp.zeros_like(acc)

        def accumulate(g):
            for d in range(1, panels):
                prim_copy(g, d).wait_recv()
            prim_local(g).wait()
            n = 0
            for i in range(panels):
                for j in range(i + 1):
                    acc[n * width : (n + 1) * width, :] += lax.dot_general(
                        prim[g, j],
                        prim[g, i],
                        (((0,), (0,)), ((), ())),
                        preferred_element_type=jnp.float32,
                    )
                    n += 1

        def both(n, carry):
            accumulate(groups // 2 + n)
            accumulate(groups // 2 - 1 - n)
            return carry

        lax.fori_loop(0, groups // 2 - 1, both, 0)
        accumulate(groups - 1)
        accumulate(0)

        side, quad = lax.rem(me, 2), me // 2
        other = 1 - side
        quad_at = [lax.rem(quad + d, quads) for d in range(quads)]
        slots = iter(range(2 + 2 * (quads - 1) + 2 * (panels - 1)))

        def span(at, size):
            return pl.ds(pl.multiple_of(at, 16), size)

        def gram_copy(source, target, device):
            slot = next(slots)
            copy = remote(source, target, gram_send.at[slot], gram_recv.at[slot], device)
            copy.start()
            return copy

        swap = gram_copy(acc.at[span(other * part, part)], arrived, {"row": quad * 2 + other})
        mirror(0, first_part)
        for g in range(mirrored):
            sec_local(g).start()
        swap.wait()
        for d in range(1, quads):
            at = quad_at[d] * slab
            outgoing[d - 1] = (
                (acc[span(side * part + at, slab), :] + arrived[span(at, slab), :])
                * (1.0 / total_rows)
            ).astype(jnp.bfloat16)
        copies = [
            gram_copy(outgoing.at[d - 1], near.at[d - 1], {"row": quad_at[d] * 2 + side})
            for d in range(1, quads)
        ]
        at = quad * slab
        total[...] = (acc[span(side * part + at, slab), :] + arrived[span(at, slab), :]) * (
            1.0 / total_rows
        )
        for d in range(1, quads):
            copies[d - 1].wait()
            total[...] += near[d - 1].astype(jnp.float32)

        thin[...] = total[...].astype(jnp.bfloat16)
        copies = [
            gram_copy(thin.at[span(vec_at[d] * height, height)], far.at[d - 1], {"vec": vec_at[d]})
            for d in range(1, panels)
        ]
        reduced = total[span(vec * height, height), :]
        for d in range(1, panels):
            copies[d - 1].wait()
            reduced += far[d - 1].astype(jnp.float32)
        at = side * part + quad * slab
        mine = span(at + vec * height, height)
        summed[mine, :] = reduced.astype(jnp.bfloat16)
        mine = summed.at[mine]
        copies = [gram_copy(mine, mine, {"vec": place}) for place in vec_at[1:]]
        for copy in copies:
            copy.wait()
        mirror(first_part, len(mirror_order))
        mine = summed.at[span(at, slab)]
        copies = [gram_copy(mine, mine, {"row": place * 2 + side}) for place in quad_at[1:]]
        for copy in copies:
            copy.wait()
        mine = summed.at[span(side * part, part)]
        gram_copy(mine, mine, {"row": quad * 2 + other}).wait()

        diagonal = lax.broadcasted_iota(jnp.int32, (width, width), 0) == lax.broadcasted_iota(
            jnp.int32, (width, width), 1
        )
        trace = jnp.zeros((1, 1), jnp.float32)
        for i in range(panels):
            n = i * (i + 1) // 2 + i
            block = summed[n * width : (n + 1) * width, :].astype(jnp.float32)
            trace += jnp.sum(jnp.where(diagonal, block, 0.0), axis=(0, 1), keepdims=True)
        scale = spectral_ref[0] * trace / float(full)
        rest, factor = scale, jnp.ones((1, 1), jnp.float32)
        for k in (64, 32, 16, 8, 4, 2, 1):
            up, down = 2.0**k, 2.0**-k
            big = rest >= up
            rest, factor = jnp.where(big, rest * down, rest), jnp.where(big, factor * down, factor)
            small = rest < down
            rest, factor = jnp.where(small, rest * up, rest), jnp.where(small, factor * up, factor)
        inverse = 1.0 / rest
        shrink = 1.0 / jnp.sqrt(scale)
        n = 0
        for i in range(panels):
            for j in range(i + 1):
                wide = summed[n * width : (n + 1) * width, :].astype(jnp.float32) * factor
                n += 1
                gram[j * width : (j + 1) * width, i * width : (i + 1) * width] = wide.astype(
                    jnp.bfloat16
                )
                if i != j:
                    gram[i * width : (i + 1) * width, j * width : (j + 1) * width] = (
                        wide.T.astype(jnp.bfloat16)
                    )

        def squares(r, carry):
            rows = pl.ds(pl.multiple_of(r * width, width), width)
            square = jnp.dot(gram[rows, :], gram[...], preferred_element_type=jnp.float32)
            square = square * inverse * inverse
            system = gram[rows, :].astype(jnp.float32) * inverse
            high[rows, :] = square.astype(jnp.bfloat16)
            low_side[rows, :] = (0.0625 * square - 0.5625 * system).astype(jnp.bfloat16)
            ones = lax.broadcasted_iota(jnp.int32, (width, full), 0) + r * width
            ones = ones == lax.broadcasted_iota(jnp.int32, (width, full), 1)
            base[rows, :] = jnp.where(ones, 2.25, 0.0) - 2.4375 * system + 1.6875 * square
            return carry

        lax.fori_loop(0, panels, squares, 0)

        def products(r, carry):
            rows = pl.ds(pl.multiple_of(r * width, width), width)
            product = jnp.dot(high[rows, :], low_side[...], preferred_element_type=jnp.float32)
            root = (base[rows, :] + product) * shrink
            for v in range(panels):
                weights[v, rows, :] = root[:, v * width : (v + 1) * width].astype(jnp.bfloat16)
            return carry

        lax.fori_loop(0, panels, products, 0)

        def product(chunk, place):
            value = None
            for u in range(panels):
                term = jnp.dot(
                    chunk[u],
                    weights[place, u * width : (u + 1) * width, :],
                    preferred_element_type=jnp.float32,
                )
                value = term if value is None else value + term
            return value.astype(jnp.bfloat16)

        hops = across + mates[1:]

        def back_copy(g, k):
            slot = (g - mirrored) * (panels - 1) + k
            return remote(
                even.at[rows_of(slot)],
                out_ref.at[rows_of(g * panels + vec)],
                back_send.at[slot],
                back_recv.at[slot],
                {"vec": hops[k]},
            )

        plain_slots = (groups - mirrored) * (panels - 1)

        def plain_local(g):
            return pltpu.make_async_copy(
                even.at[rows_of(plain_slots + g - mirrored)],
                out_ref.at[rows_of(g * panels + vec)],
                plain_keep.at[g - mirrored],
            )

        def plain_task(g):
            chunk = prim.at[g]
            for k in range(panels - 1):
                slot = (g - mirrored) * (panels - 1) + k
                even[rows_of(slot), :] = product(chunk, hops[k])
                back_copy(g, k).start()
            even[rows_of(plain_slots + g - mirrored), :] = product(chunk, vec)
            plain_local(g).start()

        held_slots = (groups - mirrored) * panels
        mate_slots = held_slots + 2 * mirrored * (half - 1)

        def mate_copy(g, role, e):
            place = g * panels + (panels - 1 - vec if role else vec)
            slot = (role * mirrored + g) * (half - 1) + e - 1
            return remote(
                even.at[rows_of(held_slots + slot)],
                out_ref.at[rows_of(place)],
                mate_send.at[slot],
                mate_recv.at[slot],
                {"vec": mates[e]},
            )

        def mate_local(g, role):
            place = g * panels + (panels - 1 - vec if role else vec)
            return pltpu.make_async_copy(
                even.at[rows_of(mate_slots + role * mirrored + g)],
                out_ref.at[rows_of(place)],
                mate_keep.at[role * mirrored + g],
            )

        def mirror_task(g, role):
            chunk = sec.at[g] if role else prim.at[g]
            if role:
                for d in range(1, panels):
                    sec_copy(g, d).wait_recv()
                sec_local(g).wait()
            for e in range(1, half):
                slot = (role * mirrored + g) * (half - 1) + e - 1
                even[rows_of(held_slots + slot), :] = product(chunk, mates[e])
                mate_copy(g, role, e).start()
            even[rows_of(mate_slots + role * mirrored + g), :] = product(chunk, vec)
            mate_local(g, role).start()

        plain = groups - mirrored
        shared = min(plain, mirrored)

        def first_round(n, carry):
            plain_task(mirrored + n)
            mirror_task(n, 0)
            return carry

        lax.fori_loop(0, shared, first_round, 0)

        def second_round(n, carry):
            plain_task(mirrored + shared + n)
            mirror_task(n, 1)
            return carry

        again = min(plain - shared, mirrored)
        lax.fori_loop(0, again, second_round, 0)

        def only_plain(n, carry):
            plain_task(n)
            return carry

        lax.fori_loop(mirrored + shared + again, groups, only_plain, 0)

        def only_mirror(n, carry):
            mirror_task(n, 1)
            return carry

        lax.fori_loop(again, mirrored, only_mirror, 0)

        def close_prim(g, carry):
            for d in range(1, panels):
                prim_copy(g, d).wait_send()
            return carry

        lax.fori_loop(0, groups, close_prim, 0)

        def close_mirror(g, carry):
            for d in range(1, panels):
                sec_copy(g, d).wait_send()
            for role in range(2):
                for e in range(1, half):
                    mate_copy(g, role, e).wait()
                mate_local(g, role).wait()
            return carry

        lax.fori_loop(0, mirrored, close_mirror, 0)

        def close_back(g, carry):
            for k in range(panels - 1):
                back_copy(g, k).wait()
            plain_local(g).wait()
            return carry

        lax.fori_loop(mirrored, groups, close_back, 0)

    square = (full, full)
    pl.run_scoped(
        basis_scope,
        pltpu.VMEM((packed, width), jnp.float32),
        pltpu.VMEM((quads - 1, slab, width), jnp.bfloat16),
        pltpu.VMEM((slab, width), jnp.float32),
        pltpu.VMEM((slab, width), jnp.bfloat16),
        pltpu.VMEM(square, jnp.bfloat16),
        pltpu.VMEM(square, jnp.bfloat16),
        pltpu.VMEM(square, jnp.bfloat16),
        pltpu.VMEM(square, jnp.float32),
        pltpu.VMEM((panels, full, width), jnp.bfloat16),
    )


def local(ham_tiles, tile_columns, stack_lengths, start_vectors, spectral_scale):
    block_count, _, tile, _ = ham_tiles.shape
    rows, width = start_vectors.shape
    count, panels = lax.axis_size("row"), lax.axis_size("vec")
    pair = REACH * tile
    pairs = block_count // REACH
    groups = pairs // panels
    mirrored = mirrored_groups(groups)
    quads, half = count // 2, panels // 2
    packed = packed_rows(panels, width, count)
    part = packed // 2
    slab = part // quads
    height = slab // panels
    smem = pl.BlockSpec(memory_space=pltpu.SMEM)
    hbm = pl.BlockSpec(memory_space=pl.ANY)
    gram_copies = 2 + 2 * (quads - 1) + 2 * (panels - 1)
    back = (groups - mirrored) * (panels - 1)
    mate = 2 * mirrored * (half - 1)
    dma = pltpu.SemaphoreType.DMA
    return pl.pallas_call(
        functools.partial(step_kernel, block_count * count, rows * count),
        out_shape=jax.ShapeDtypeStruct((rows, width), jnp.bfloat16),
        in_specs=[smem, smem, smem, hbm, hbm],
        out_specs=pl.BlockSpec(memory_space=pltpu.HBM),
        scratch_shapes=[
            pltpu.VMEM((rows, width), jnp.bfloat16),
            pltpu.VMEM((rows, width), jnp.bfloat16),
            pltpu.VMEM((rows, width), jnp.bfloat16),
            pltpu.VMEM((rows, width), jnp.bfloat16),
            pltpu.VMEM((CHEB, 2, pair, width), jnp.bfloat16),
            pltpu.VMEM((groups, panels, pair, width), jnp.bfloat16),
            pltpu.VMEM((mirrored, panels, pair, width), jnp.bfloat16),
            pltpu.VMEM((part, width), jnp.float32),
            pltpu.VMEM((quads - 1, slab, width), jnp.bfloat16),
            pltpu.VMEM((panels - 1, height, width), jnp.bfloat16),
            pltpu.VMEM((packed, width), jnp.bfloat16),
            dma((8,)),
            dma((CHEB, 2)),
            dma((CHEB, 2)),
            dma((groups, panels - 1)),
            dma((groups, panels - 1)),
            dma((groups,)),
            dma((mirrored, panels - 1)),
            dma((mirrored, panels - 1)),
            dma((mirrored,)),
            dma((gram_copies,)),
            dma((gram_copies,)),
            dma((back,)),
            dma((back,)),
            dma((groups - mirrored,)),
            dma((mate,)),
            dma((mate,)),
            dma((2 * mirrored,)),
        ],
        compiler_params=pltpu.CompilerParams(
            collective_id=0, has_side_effects=True, vmem_limit_bytes=47 * 1024 * 1024
        ),
    )(tile_columns.T, stack_lengths, spectral_scale, ham_tiles, start_vectors)


def solution(mesh):
    placed = (P("row", None, None, None), P("row", None), P("row"), P("row", "vec"), P())
    return jax.shard_map(
        local, mesh=mesh, in_specs=placed, out_specs=P("row", "vec"), check_vma=False
    )
```

```python
import functools

import jax
import jax.numpy as jnp
from jax import lax
from jax.experimental import pallas as pl
from jax.experimental.pallas import tpu as pltpu
from jax.sharding import PartitionSpec as P

REACH = 2
CHEB = 6
MESH = pl.DeviceIdType.MESH


def packed_rows(panels, width, count):
    unit = 16 * count * panels
    return -(-(panels * (panels + 1) // 2 * width) // unit) * unit


def mirrored_groups(groups):
    return groups * 3 // 8


def step_kernel(
    total_blocks,
    total_rows,
    columns_ref,
    lengths_ref,
    spectral_ref,
    tiles_hbm,
    start_hbm,
    out_ref,
    start,
    even,
    odd,
    final,
    halo,
    prim,
    sec,
    arrived,
    near,
    far,
    summed,
    load_sem,
    halo_send,
    halo_recv,
    prim_send,
    prim_recv,
    prim_keep,
    sec_send,
    sec_recv,
    sec_keep,
    gram_send,
    gram_recv,
    back_send,
    back_recv,
    plain_keep,
    mate_send,
    mate_recv,
    mate_keep,
):
    block_count, tile_count, tile, _ = tiles_hbm.shape
    groups, panels, pair, width = prim.shape
    mirrored = sec.shape[0]
    pairs = groups * panels
    half = panels // 2
    full = panels * width
    count = lax.axis_size("row")
    me, vec = lax.axis_index("row"), lax.axis_index("vec")
    left, right = lax.rem(me + count - 1, count), lax.rem(me + 1, count)
    vec_at = [lax.rem(vec + d, panels) for d in range(panels)]
    upper, low = vec // half, lax.rem(vec, half)
    mates = [upper * half + lax.rem(low + e, half) for e in range(half)]
    across = [(1 - upper) * half + lax.rem(low + e, half) for e in range(half)]
    c = pairs // 2
    spare = c - 2 * CHEB
    part, quads = arrived.shape[0], count // 2
    packed, slab = 2 * part, part // quads
    height = slab // panels

    def rows_of(p):
        return pl.ds(pl.multiple_of(p * pair, pair), pair)

    def remote(source, target, send, recv, device):
        return pltpu.make_async_remote_copy(
            src_ref=source,
            dst_ref=target,
            send_sem=send,
            recv_sem=recv,
            device_id=device,
            device_id_type=MESH,
        )

    barrier = pltpu.get_barrier_semaphore()
    greeted = [{"row": lax.rem(me + d, count)} for d in range(1, count)]
    greeted += [{"vec": place} for place in vec_at[1:]]
    for device in greeted:
        pl.semaphore_signal(barrier, inc=1, device_id=device, device_id_type=MESH)

    def halo_copies(source, step):
        return (
            remote(
                source.at[pl.ds(0, pair)],
                halo.at[step, 1],
                halo_send.at[step, 1],
                halo_recv.at[step, 1],
                {"row": left},
            ),
            remote(
                source.at[pl.ds((pairs - 1) * pair, pair)],
                halo.at[step, 0],
                halo_send.at[step, 0],
                halo_recv.at[step, 0],
                {"row": right},
            ),
        )

    def prim_copy(g, d):
        return remote(
            final.at[rows_of(g * panels + vec_at[d])],
            prim.at[g, vec],
            prim_send.at[g, d - 1],
            prim_recv.at[g, d - 1],
            {"vec": vec_at[d]},
        )

    def prim_local(g):
        return pltpu.make_async_copy(
            final.at[rows_of(g * panels + vec)], prim.at[g, vec], prim_keep.at[g]
        )

    def send_chunk(p):
        g, owner = p // panels, lax.rem(p, panels)
        d = lax.rem(owner - vec + panels, panels)

        @pl.when(d != 0)
        def _():
            remote(
                final.at[rows_of(p)],
                prim.at[g, vec],
                prim_send.at[g, d - 1],
                prim_recv.at[g, d - 1],
                {"vec": owner},
            ).start()

        @pl.when(d == 0)
        def _():
            prim_local(g).start()

    mirror_order = [(g, d) for g in range(mirrored) for d in range(1, panels)]
    first_part = panels - 1

    def sec_copy(g, d):
        return remote(
            final.at[rows_of(g * panels + panels - 1 - vec_at[d])],
            sec.at[g, vec],
            sec_send.at[g, d - 1],
            sec_recv.at[g, d - 1],
            {"vec": vec_at[d]},
        )

    def sec_local(g):
        return pltpu.make_async_copy(
            final.at[rows_of(g * panels + panels - 1 - vec)], sec.at[g, vec], sec_keep.at[g]
        )

    def mirror(lo, hi):
        for g, d in mirror_order[lo:hi]:
            sec_copy(g, d).start()

    def filter_scope(tiles, band):
        def tile_load(n, lo, hi, slot):
            return pltpu.make_async_copy(
                tiles_hbm.at[pl.ds(lo * REACH, (hi - lo) * REACH)],
                tiles.at[pl.ds(slot * REACH, (hi - lo) * REACH)],
                load_sem.at[n],
            )

        def start_load(n, lo, hi):
            piece = pl.ds(lo * pair, (hi - lo) * pair)
            return pltpu.make_async_copy(start_hbm.at[piece], start.at[piece], load_sem.at[n])

        first = [
            tile_load(0, c - CHEB, c + CHEB, 0),
            start_load(1, c - CHEB - 1, c + CHEB + 1),
        ]
        rest = [
            start_load(2, 0, c - CHEB - 1),
            start_load(3, c + CHEB + 1, pairs),
            tile_load(4, CHEB, c - CHEB, 2 * CHEB),
            tile_load(5, c + CHEB, pairs - CHEB, 2 * CHEB + spare),
        ]
        ends = [tile_load(6, 0, CHEB, 0), tile_load(7, pairs - CHEB, pairs, CHEB)]
        for load in first + rest:
            load.start()

        def build(p, slot):
            for i in range(REACH):
                b = p * REACH + i
                at = slot * REACH + i
                live = (b < lengths_ref[0] - REACH) | (b >= block_count - REACH)
                places = []
                for t in range(1, tile_count):
                    shift = lax.rem(
                        columns_ref[t, b] - (me * block_count + b) + REACH + total_blocks,
                        total_blocks,
                    )
                    places.append(jnp.where(live, shift, -1))

                def masked(t, hit):
                    mask = jnp.where(hit, 1.0, 0.0).astype(jnp.float32)
                    mask = jnp.full((tile, tile), mask, jnp.float32).astype(jnp.bfloat16)
                    return tiles[at, t] * mask

                for k in range(3 * REACH):
                    if k - i == REACH:
                        value = masked(0, live)
                    elif 0 <= k - i <= 2 * REACH:
                        value = masked(1, places[0] == k - i)
                        for t in range(2, tile_count):
                            value = value + masked(t, places[t - 1] == k - i)
                    else:
                        value = jnp.zeros((tile, tile), jnp.bfloat16)
                    band[p, i * tile : (i + 1) * tile, k * tile : (k + 1) * tile] = value

        held = [start] + [(odd, even)[step % 2] for step in range(CHEB - 1)] + [final]

        def finish(step, product, rows):
            if step:
                product = 2.0 * product - held[step - 1][rows, :].astype(jnp.float32)
            held[step + 1][rows, :] = product.astype(jnp.bfloat16)

        def interior(step, p):
            before = pl.multiple_of((p - 1) * pair, pair)
            finish(
                step,
                jnp.dot(
                    band[p],
                    held[step][pl.ds(before, 3 * pair), :],
                    preferred_element_type=jnp.float32,
                ),
                rows_of(p),
            )

        for load in first:
            load.wait()

        def base(n, carry):
            for p in (c - 1 - n, c + n):
                build(p, p - (c - CHEB))
                interior(0, p)
            return carry

        lax.fori_loop(0, CHEB, base, 0)
        for load in ends:
            load.start()
        for step in range(1, CHEB):

            def layer(n, carry, step=step):
                interior(step, c - 1 - n)
                interior(step, c + n)
                return carry

            lax.fori_loop(0, CHEB - step, layer, 0)

        pl.semaphore_wait(barrier, len(greeted))
        send_chunk(c)
        send_chunk(c - 1)
        for load in rest + ends:
            load.wait()
        copies = halo_copies(start, 0)
        for copy in copies:
            copy.start()

        last = (pairs - 1) * pair

        def waves(lo, hi):
            first_step = max(0, -(-(lo - spare) // 2))

            def wave(i, carry):
                if first_step == 0:
                    build(c + CHEB - 1 + i, 2 * CHEB + spare - 1 + i)
                    build(c - CHEB - i, 2 * CHEB + spare - i)
                for step in range(first_step, CHEB):
                    interior(step, c + CHEB - 1 - step + i)
                    interior(step, c - CHEB + step - i)
                send_chunk(c + i)
                send_chunk(c - 1 - i)
                return carry

            lax.fori_loop(lo, hi, wave, 0)

        def edges(step, copies):
            current = held[step]
            if step == 0:

                def outer(p, carry):
                    build(p, p)
                    build(pairs - 1 - p, 2 * CHEB - 1 - p)
                    return carry

                lax.fori_loop(0, CHEB, outer, 0)
            for copy in copies:
                copy.wait()
            finish(
                step,
                jnp.dot(band[0, :, :pair], halo[step, 0], preferred_element_type=jnp.float32)
                + jnp.dot(
                    band[0, :, pair:], current[0 : 2 * pair, :], preferred_element_type=jnp.float32
                ),
                pl.ds(0, pair),
            )
            finish(
                step,
                jnp.dot(
                    band[pairs - 1, :, 2 * pair :],
                    halo[step, 1],
                    preferred_element_type=jnp.float32,
                )
                + jnp.dot(
                    band[pairs - 1, :, : 2 * pair],
                    current[last - pair : last + pair, :],
                    preferred_element_type=jnp.float32,
                ),
                pl.ds(last, pair),
            )
            if step == CHEB - 1:
                send_chunk(pairs - 1)
                send_chunk(0)
                return []
            copies = halo_copies(held[step + 1], step + 1)
            for copy in copies:
                copy.start()

            def sides(p, carry, step=step):
                interior(step, p)
                interior(step, pairs - 1 - p)
                return carry

            lax.fori_loop(1, CHEB - step, sides, 0)
            return copies

        waves(1, 2)
        copies = edges(0, copies)
        waves(2, spare)
        copies = edges(1, copies)
        waves(spare, spare + 1)
        for step in range(CHEB - 1):
            waves(spare + 1 + 2 * step, spare + 3 + 2 * step)
            if step + 2 < CHEB:
                copies = edges(step + 2, copies)

    pl.run_scoped(
        filter_scope,
        pltpu.VMEM((2 * (CHEB + spare) * REACH, tile_count, tile, tile), jnp.bfloat16),
        pltpu.VMEM((pairs, pair, 3 * pair), jnp.bfloat16),
    )

    def basis_scope(acc, outgoing, total, thin, gram, high, low_side, base, weights):
        acc[...] = jnp.zeros_like(acc)

        def accumulate(g):
            for d in range(1, panels):
                prim_copy(g, d).wait_recv()
            prim_local(g).wait()
            n = 0
            for i in range(panels):
                for j in range(i + 1):
                    acc[n * width : (n + 1) * width, :] += lax.dot_general(
                        prim[g, j],
                        prim[g, i],
                        (((0,), (0,)), ((), ())),
                        preferred_element_type=jnp.float32,
                    )
                    n += 1

        def both(n, carry):
            accumulate(groups // 2 + n)
            accumulate(groups // 2 - 1 - n)
            return carry

        lax.fori_loop(0, groups // 2 - 1, both, 0)
        accumulate(groups - 1)
        mirror(0, first_part)
        for g in range(mirrored):
            sec_local(g).start()
        accumulate(0)

        side, quad = lax.rem(me, 2), me // 2
        other = 1 - side
        quad_at = [lax.rem(quad + d, quads) for d in range(quads)]
        slots = iter(range(2 + 2 * (quads - 1) + 2 * (panels - 1)))

        def span(at, size):
            return pl.ds(pl.multiple_of(at, 16), size)

        def gram_copy(source, target, device):
            slot = next(slots)
            copy = remote(source, target, gram_send.at[slot], gram_recv.at[slot], device)
            copy.start()
            return copy

        gram_copy(acc.at[span(other * part, part)], arrived, {"row": quad * 2 + other}).wait()
        for d in range(1, quads):
            at = quad_at[d] * slab
            outgoing[d - 1] = (
                (acc[span(side * part + at, slab), :] + arrived[span(at, slab), :])
                * (1.0 / total_rows)
            ).astype(jnp.bfloat16)
        copies = [
            gram_copy(outgoing.at[d - 1], near.at[d - 1], {"row": quad_at[d] * 2 + side})
            for d in range(1, quads)
        ]
        at = quad * slab
        total[...] = (acc[span(side * part + at, slab), :] + arrived[span(at, slab), :]) * (
            1.0 / total_rows
        )
        for d in range(1, quads):
            copies[d - 1].wait()
            total[...] += near[d - 1].astype(jnp.float32)

        thin[...] = total[...].astype(jnp.bfloat16)
        copies = [
            gram_copy(thin.at[span(vec_at[d] * height, height)], far.at[d - 1], {"vec": vec_at[d]})
            for d in range(1, panels)
        ]
        reduced = total[span(vec * height, height), :]
        for d in range(1, panels):
            copies[d - 1].wait()
            reduced += far[d - 1].astype(jnp.float32)
        at = side * part + quad * slab
        mine = span(at + vec * height, height)
        summed[mine, :] = reduced.astype(jnp.bfloat16)
        mine = summed.at[mine]
        copies = [gram_copy(mine, mine, {"vec": place}) for place in vec_at[1:]]
        for copy in copies:
            copy.wait()
        mirror(first_part, len(mirror_order))
        mine = summed.at[span(at, slab)]
        copies = [gram_copy(mine, mine, {"row": place * 2 + side}) for place in quad_at[1:]]
        for copy in copies:
            copy.wait()
        mine = summed.at[span(side * part, part)]
        gram_copy(mine, mine, {"row": quad * 2 + other}).wait()

        diagonal = lax.broadcasted_iota(jnp.int32, (width, width), 0) == lax.broadcasted_iota(
            jnp.int32, (width, width), 1
        )
        trace = jnp.zeros((1, 1), jnp.float32)
        for i in range(panels):
            n = i * (i + 1) // 2 + i
            block = summed[n * width : (n + 1) * width, :].astype(jnp.float32)
            trace += jnp.sum(jnp.where(diagonal, block, 0.0), axis=(0, 1), keepdims=True)
        scale = spectral_ref[0] * trace / float(full)
        rest, factor = scale, jnp.ones((1, 1), jnp.float32)
        for k in (64, 32, 16, 8, 4, 2, 1):
            up, down = 2.0**k, 2.0**-k
            big = rest >= up
            rest, factor = jnp.where(big, rest * down, rest), jnp.where(big, factor * down, factor)
            small = rest < down
            rest, factor = jnp.where(small, rest * up, rest), jnp.where(small, factor * up, factor)
        inverse = 1.0 / rest
        shrink = 1.0 / jnp.sqrt(scale)
        n = 0
        for i in range(panels):
            for j in range(i + 1):
                wide = summed[n * width : (n + 1) * width, :].astype(jnp.float32) * factor
                n += 1
                gram[j * width : (j + 1) * width, i * width : (i + 1) * width] = wide.astype(
                    jnp.bfloat16
                )
                if i != j:
                    gram[i * width : (i + 1) * width, j * width : (j + 1) * width] = (
                        wide.T.astype(jnp.bfloat16)
                    )

        def squares(r, carry):
            rows = pl.ds(pl.multiple_of(r * width, width), width)
            square = jnp.dot(gram[rows, :], gram[...], preferred_element_type=jnp.float32)
            square = square * inverse * inverse
            system = gram[rows, :].astype(jnp.float32) * inverse
            high[rows, :] = square.astype(jnp.bfloat16)
            low_side[rows, :] = (0.0625 * square - 0.5625 * system).astype(jnp.bfloat16)
            ones = lax.broadcasted_iota(jnp.int32, (width, full), 0) + r * width
            ones = ones == lax.broadcasted_iota(jnp.int32, (width, full), 1)
            base[rows, :] = jnp.where(ones, 2.25, 0.0) - 2.4375 * system + 1.6875 * square
            return carry

        lax.fori_loop(0, panels, squares, 0)

        def products(r, carry):
            rows = pl.ds(pl.multiple_of(r * width, width), width)
            product = jnp.dot(high[rows, :], low_side[...], preferred_element_type=jnp.float32)
            root = (base[rows, :] + product) * shrink
            for v in range(panels):
                weights[v, rows, :] = root[:, v * width : (v + 1) * width].astype(jnp.bfloat16)
            return carry

        lax.fori_loop(0, panels, products, 0)

        def product(chunk, place):
            value = None
            for u in range(panels):
                term = jnp.dot(
                    chunk[u],
                    weights[place, u * width : (u + 1) * width, :],
                    preferred_element_type=jnp.float32,
                )
                value = term if value is None else value + term
            return value.astype(jnp.bfloat16)

        hops = across[:1] + mates[1:] + across[1:]

        def back_copy(g, k):
            slot = (g - mirrored) * (panels - 1) + k
            return remote(
                even.at[rows_of(slot)],
                out_ref.at[rows_of(g * panels + vec)],
                back_send.at[slot],
                back_recv.at[slot],
                {"vec": hops[k]},
            )

        plain_slots = (groups - mirrored) * (panels - 1)

        def plain_local(g):
            return pltpu.make_async_copy(
                even.at[rows_of(plain_slots + g - mirrored)],
                out_ref.at[rows_of(g * panels + vec)],
                plain_keep.at[g - mirrored],
            )

        def plain_task(g):
            chunk = prim.at[g]
            for k in range(panels - 1):
                slot = (g - mirrored) * (panels - 1) + k
                even[rows_of(slot), :] = product(chunk, hops[k])
                back_copy(g, k).start()
            even[rows_of(plain_slots + g - mirrored), :] = product(chunk, vec)
            plain_local(g).start()

        held_slots = (groups - mirrored) * panels
        mate_slots = held_slots + 2 * mirrored * (half - 1)

        def mate_copy(g, role, e):
            place = g * panels + (panels - 1 - vec if role else vec)
            slot = (role * mirrored + g) * (half - 1) + e - 1
            return remote(
                even.at[rows_of(held_slots + slot)],
                out_ref.at[rows_of(place)],
                mate_send.at[slot],
                mate_recv.at[slot],
                {"vec": mates[e]},
            )

        def mate_local(g, role):
            place = g * panels + (panels - 1 - vec if role else vec)
            return pltpu.make_async_copy(
                even.at[rows_of(mate_slots + role * mirrored + g)],
                out_ref.at[rows_of(place)],
                mate_keep.at[role * mirrored + g],
            )

        def mirror_task(g, role):
            chunk = sec.at[g] if role else prim.at[g]
            if role:
                for d in range(1, panels):
                    sec_copy(g, d).wait_recv()
                sec_local(g).wait()
            for e in range(1, half):
                slot = (role * mirrored + g) * (half - 1) + e - 1
                even[rows_of(held_slots + slot), :] = product(chunk, mates[e])
                mate_copy(g, role, e).start()
            even[rows_of(mate_slots + role * mirrored + g), :] = product(chunk, vec)
            mate_local(g, role).start()

        plain = groups - mirrored
        shared = min(plain, mirrored)

        def first_round(n, carry):
            plain_task(mirrored + n)
            mirror_task(n, 0)
            return carry

        lax.fori_loop(0, shared, first_round, 0)

        def second_round(n, carry):
            plain_task(mirrored + shared + n)
            mirror_task(n, 1)
            return carry

        again = min(plain - shared, mirrored)
        lax.fori_loop(0, again, second_round, 0)

        def only_plain(n, carry):
            plain_task(n)
            return carry

        lax.fori_loop(mirrored + shared + again, groups, only_plain, 0)

        def only_mirror(n, carry):
            mirror_task(n, 1)
            return carry

        lax.fori_loop(again, mirrored, only_mirror, 0)

        def close_prim(g, carry):
            for d in range(1, panels):
                prim_copy(g, d).wait_send()
            return carry

        lax.fori_loop(0, groups, close_prim, 0)

        def close_mirror(g, carry):
            for d in range(1, panels):
                sec_copy(g, d).wait_send()
            for role in range(2):
                for e in range(1, half):
                    mate_copy(g, role, e).wait()
                mate_local(g, role).wait()
            return carry

        lax.fori_loop(0, mirrored, close_mirror, 0)

        def close_back(g, carry):
            for k in range(panels - 1):
                back_copy(g, k).wait()
            plain_local(g).wait()
            return carry

        lax.fori_loop(mirrored, groups, close_back, 0)

    square = (full, full)
    pl.run_scoped(
        basis_scope,
        pltpu.VMEM((packed, width), jnp.float32),
        pltpu.VMEM((quads - 1, slab, width), jnp.bfloat16),
        pltpu.VMEM((slab, width), jnp.float32),
        pltpu.VMEM((slab, width), jnp.bfloat16),
        pltpu.VMEM(square, jnp.bfloat16),
        pltpu.VMEM(square, jnp.bfloat16),
        pltpu.VMEM(square, jnp.bfloat16),
        pltpu.VMEM(square, jnp.float32),
        pltpu.VMEM((panels, full, width), jnp.bfloat16),
    )


def local(ham_tiles, tile_columns, stack_lengths, start_vectors, spectral_scale):
    block_count, _, tile, _ = ham_tiles.shape
    rows, width = start_vectors.shape
    count, panels = lax.axis_size("row"), lax.axis_size("vec")
    pair = REACH * tile
    pairs = block_count // REACH
    groups = pairs // panels
    mirrored = mirrored_groups(groups)
    quads, half = count // 2, panels // 2
    packed = packed_rows(panels, width, count)
    part = packed // 2
    slab = part // quads
    height = slab // panels
    smem = pl.BlockSpec(memory_space=pltpu.SMEM)
    hbm = pl.BlockSpec(memory_space=pl.ANY)
    gram_copies = 2 + 2 * (quads - 1) + 2 * (panels - 1)
    back = (groups - mirrored) * (panels - 1)
    mate = 2 * mirrored * (half - 1)
    dma = pltpu.SemaphoreType.DMA
    return pl.pallas_call(
        functools.partial(step_kernel, block_count * count, rows * count),
        out_shape=jax.ShapeDtypeStruct((rows, width), jnp.bfloat16),
        in_specs=[smem, smem, smem, hbm, hbm],
        out_specs=pl.BlockSpec(memory_space=pltpu.HBM),
        scratch_shapes=[
            pltpu.VMEM((rows, width), jnp.bfloat16),
            pltpu.VMEM((rows, width), jnp.bfloat16),
            pltpu.VMEM((rows, width), jnp.bfloat16),
            pltpu.VMEM((rows, width), jnp.bfloat16),
            pltpu.VMEM((CHEB, 2, pair, width), jnp.bfloat16),
            pltpu.VMEM((groups, panels, pair, width), jnp.bfloat16),
            pltpu.VMEM((mirrored, panels, pair, width), jnp.bfloat16),
            pltpu.VMEM((part, width), jnp.float32),
            pltpu.VMEM((quads - 1, slab, width), jnp.bfloat16),
            pltpu.VMEM((panels - 1, height, width), jnp.bfloat16),
            pltpu.VMEM((packed, width), jnp.bfloat16),
            dma((8,)),
            dma((CHEB, 2)),
            dma((CHEB, 2)),
            dma((groups, panels - 1)),
            dma((groups, panels - 1)),
            dma((groups,)),
            dma((mirrored, panels - 1)),
            dma((mirrored, panels - 1)),
            dma((mirrored,)),
            dma((gram_copies,)),
            dma((gram_copies,)),
            dma((back,)),
            dma((back,)),
            dma((groups - mirrored,)),
            dma((mate,)),
            dma((mate,)),
            dma((2 * mirrored,)),
        ],
        compiler_params=pltpu.CompilerParams(
            collective_id=0, has_side_effects=True, vmem_limit_bytes=47 * 1024 * 1024
        ),
    )(tile_columns.T, stack_lengths, spectral_scale, ham_tiles, start_vectors)


def solution(mesh):
    placed = (P("row", None, None, None), P("row", None), P("row"), P("row", "vec"), P())
    return jax.shard_map(
        local, mesh=mesh, in_specs=placed, out_specs=P("row", "vec"), check_vma=False
    )
```
